1024 devices in a mesh: ctx: 16 (over y, z_lo), section: 8 (over x), tp: 8 (over z_hi, core).
Axes of the slice: x: 8, y: 8, z: 8 (z_hi: 4, z_lo: 2; z = z_hi * 2 + z_lo), core: 2. Of those that a mesh axis runs over, the one named last changes fastest.
Arguments:
- row_offsets: int32 [8], P('section'), may hold values from 7552 to 8192
- queries: bfloat16 [8, 2048, 4096], P('section', 'ctx', 'tp'), may hold values from -8 to 8
- cache_keys: bfloat16 [8, 10240, 1024], P('section', 'ctx', 'tp'), may hold values from -4 to 4
- cache_values: bfloat16 [8, 10240, 1024], P('section', 'ctx', 'tp'), may hold values from -6 to 6
- residual: bfloat16 [8, 2048, 5120], P('section', 'ctx', 'tp'), may hold values from -6 to 6
- out_weight: bfloat16 [8, 4096, 5120], P('section', 'tp'), may hold values from -0.09375 to 0.09375
Outputs:
- next_inputs: bfloat16 [8, 2048, 5120], P('section', 'ctx', 'tp')
The draws below stay inside these ranges and needn't reach their ends.
All inputs are finite; a program needn't handle non-finite values.
Results may differ from the reference program's by a relative error of at most 0.0085.
Values may be sent and summed in bfloat16 or wider, within the bound.
A program may use at most 32 MiB of HBM per device.

```python
import jax
import jax.numpy as jnp
from jax import lax

D = 5120
H = 32
KVH = 8
HD = 128
G = 4
S_LOC = 640
MICRO = 8
ROWS = 2048
CACHE = 10240
N_TP = 8


def draw_queries(key, part):
    base_key = jax.random.fold_in(key, 11)
    sample = 2.0 * jax.random.normal(jax.random.fold_in(base_key, 3), (MICRO, ROWS, H * HD), jnp.float32)
    sample = jnp.clip(sample, -8.0, 8.0)
    return sample.astype(jnp.bfloat16)


def draw_cache_keys(key, part):
    base_key = jax.random.fold_in(key, 23)
    sample = jax.random.normal(jax.random.fold_in(base_key, 3), (MICRO, CACHE, KVH * HD), jnp.float32)
    sample = jnp.clip(sample, -4.0, 4.0)
    return sample.astype(jnp.bfloat16)


def place_ends(values, rng, smallest, largest):
    longest = values.shape.index(max(values.shape))
    spots = []
    for shift in (0, 1):
        where = [jax.random.randint(jax.random.fold_in(rng, axis), (), 0, length) for axis, length in enumerate(values.shape)]
        where[longest] = (where[longest] + shift) % values.shape[longest]
        spots.append(tuple(where))
    return values.at[spots[0]].set(smallest).at[spots[1]].set(largest)


def shard_levels(key, dims, cuts, low, largest):
    level, own = 1.0, jax.random.fold_in(key, 6)
    for dim, parts in cuts:
        heights = jnp.exp(jax.random.uniform(jax.random.fold_in(own, dim), (parts,), jnp.float32, low / len(cuts), largest / len(cuts)))
        level = level * jnp.repeat(heights, dims[dim] // parts).reshape([-1 if axis == dim else 1 for axis in range(len(dims))])
    return level


def centred(stream_key, extent, width, limit, shards=(), kind=jnp.bfloat16):
    gain = shard_levels(stream_key, extent, shards, -0.22, 0.18) if shards else 1.0
    values = jax.random.normal(stream_key, extent, jnp.float32) * width * gain
    return jnp.minimum(jnp.maximum(values, -limit), limit).astype(kind)


def setup_inputs(seed: int = 0) -> dict:
    keys = jax.random.split(jax.random.key(seed), 7)
    return {
        "row_offsets": place_ends(jax.random.randint(keys[0], (MICRO,), CACHE - ROWS - S_LOC, CACHE - ROWS + 1), jax.random.fold_in(keys[0], 1), CACHE - ROWS - S_LOC, CACHE - ROWS).astype(jnp.int32),
        "queries": draw_queries(jax.random.fold_in(keys[6], 71), 0),
        "cache_keys": draw_cache_keys(jax.random.fold_in(keys[6], 71), 0),
        "cache_values": centred(keys[3], (MICRO, CACHE, KVH * HD), 1.0, 6.0, ((0, 8), (1, 16), (2, 8))),
        "residual": centred(keys[4], (MICRO, ROWS, D), 1.0, 6.0, ((0, 8), (1, 16), (2, 8))),
        "out_weight": centred(keys[5], (MICRO, H * HD, D), (H * HD) ** -0.5, 0.09375, ((0, 8), (1, 8))),
    }


def attend_section(offset, query_rows, key_rows, value_rows):
    query_heads = query_rows.reshape(ROWS, KVH, G, HD).transpose(1, 0, 2, 3)
    key_heads = key_rows.reshape(CACHE, KVH, HD).transpose(1, 0, 2)
    value_heads = value_rows.reshape(CACHE, KVH, HD).transpose(1, 0, 2)
    query_pos = offset + jnp.arange(ROWS, dtype=jnp.int32)
    key_pos = jnp.arange(CACHE, dtype=jnp.int32)
    visible = key_pos[None, :] <= query_pos[:, None]

    def one_group(operands):
        query_group, key_group, value_group = operands
        scores = jnp.einsum("qgd,sd->gqs", query_group.astype(jnp.float32), key_group.astype(jnp.float32)) * (HD ** -0.5)
        scores = jnp.where(visible[None], scores, -jnp.inf)
        row_max = jnp.max(scores, axis=-1, keepdims=True)
        weights = jnp.where(visible[None], jnp.exp(scores - row_max), 0.0)
        row_sum = jnp.sum(weights, axis=-1, keepdims=True)
        rounded = lax.optimization_barrier(weights.astype(jnp.bfloat16)).astype(jnp.float32)
        mixed = jnp.einsum("gqs,sd->gqd", rounded, value_group.astype(jnp.float32))
        return mixed / row_sum

    result = lax.map(one_group, (query_heads, key_heads, value_heads))
    return result.transpose(2, 0, 1, 3).reshape(ROWS, H * HD).astype(jnp.bfloat16)


def reference(row_offsets, queries, cache_keys, cache_values, residual, out_weight):
    group_width = H * HD // N_TP
    outputs = []
    for section_index in range(MICRO):
        attended = attend_section(row_offsets[section_index], queries[section_index], cache_keys[section_index], cache_values[section_index])
        projected = jnp.zeros((ROWS, D), jnp.float32)
        for group_index in range(N_TP):
            lower = group_index * group_width
            upper = lower + group_width
            partial_term = jnp.dot(attended[:, lower:upper], out_weight[section_index, lower:upper], preferred_element_type=jnp.float32)
            projected = projected + lax.optimization_barrier(partial_term.astype(jnp.bfloat16)).astype(jnp.float32)
        outputs.append((residual[section_index].astype(jnp.float32) + projected).astype(jnp.bfloat16))
    return jnp.roll(jnp.stack(outputs), 1, axis=0)
```

```python
import functools

import jax
import jax.numpy as jnp
from jax import lax
from jax.experimental import pallas as pl
from jax.experimental.pallas import tpu as pltpu
from jax.sharding import PartitionSpec as P

HD = 128
G = 4
NEG = -(2.0**100)
LOG2E = 1.4426950408889634
AHEAD = 3
PARTS = 2
MESH = pl.DeviceIdType.MESH
BF = jnp.bfloat16
F32 = jnp.float32


def kernel(
    ny, nzh, nx,
    off_ref, q_ref, k_ref, v_ref, res_ref, w_ref, o_ref,
    kbuf, vbuf, vt, qb, snd, rcv, att, wbuf, keep, base,
    far_s, far_r, near_s, near_r, mix_s, mix_r, fin,
    kv_l, kv_s, kv_r, q_l, q_s, q_r, a_s, a_r, w_l, w_s, w_r, t_s, t_r,
    far_ss, far_rs, near_ss, near_rs, mix_ss, mix_rs, x_s, x_r,
):
    rows = q_ref.shape[0]
    klen = k_ref.shape[0]
    width = res_ref.shape[1]
    half = rows // 2
    part = half // PARTS
    two = 2 * HD

    ctx = lax.axis_index("ctx")
    tp = lax.axis_index("tp")
    x = lax.axis_index("section")
    y, zl = ctx // 2, ctx % 2
    zh, co = tp // 2, tp % 2
    y_next = {"ctx": ((y + 1) % ny) * 2 + zl}
    y_prev = {"ctx": ((y + ny - 1) % ny) * 2 + zl}
    ring = (y_next, y_prev)
    z_mate = {"ctx": y * 2 + 1 - zl}
    core_mate = {"tp": zh * 2 + 1 - co}
    zh_next = {"tp": ((zh + 1) % nzh) * 2 + co}
    zh_prev = {"tp": ((zh + nzh - 1) % nzh) * 2 + co}
    zring = (zh_next, zh_prev)
    x_next = {"section": (x + 1) % nx}
    x_prev = {"section": (x + nx - 1) % nx}

    def remote(src, dst, s, r, where):
        return pltpu.make_async_remote_copy(
            src_ref=src, dst_ref=dst, send_sem=s, recv_sem=r, device_id=where, device_id_type=MESH
        )

    def wcols(block, core):
        return pl.ds(pl.multiple_of(block * 2 * width + core * width, width), width)

    own_rows = pl.ds(pl.multiple_of(zl * klen, klen), klen)
    local_k = pltpu.make_async_copy(k_ref, kbuf.at[own_rows], kv_l.at[0])
    local_v = pltpu.make_async_copy(v_ref, vbuf.at[own_rows], kv_l.at[1])
    local_q = [
        pltpu.make_async_copy(q_ref.at[:, pl.ds(d * two, two)], qb.at[d, ny - 1], q_l.at[d]) for d in (0, 1)
    ]
    local_w = [
        pltpu.make_async_copy(w_ref.at[:, wcols(b, co)], wbuf.at[b, co], w_l.at[b]) for b in range(nzh)
    ]
    local_k.start()
    local_v.start()
    for c in local_q:
        c.start()

    barrier = pltpu.get_barrier_semaphore()
    greet = (y_next, y_prev, z_mate, core_mate, zh_next, zh_prev, x_next, x_prev)
    for where in greet:
        pl.semaphore_signal(barrier, inc=1, device_id=where, device_id_type=MESH)
    pl.semaphore_wait(barrier, len(greet))

    send_k = remote(k_ref, kbuf.at[own_rows], kv_s.at[0], kv_r.at[0], z_mate)
    send_v = remote(v_ref, vbuf.at[own_rows], kv_s.at[1], kv_r.at[1], z_mate)
    send_k.start()
    send_v.start()
    for d in (0, 1):
        remote(
            q_ref.at[:, pl.ds(d * two, two)], qb.at[d, 0], q_s.at[d, 0], q_r.at[d, 0], ring[d]
        ).start()

    def q_hop(d, slot):
        return remote(qb.at[d, slot], qb.at[d, slot + 1], q_s.at[d, slot + 1], q_r.at[d, slot + 1], ring[d])

    def q_arrival(d, slot):
        return remote(qb.at[d, slot], qb.at[d, slot], q_s.at[d, slot], q_r.at[d, slot], ring[d])

    send_w = [
        remote(w_ref.at[:, wcols(b, 1 - co)], wbuf.at[b, co], w_s.at[b], w_r.at[b], core_mate)
        for b in range(nzh)
    ]
    for c in local_w:
        c.start()
    for c in send_w:
        c.start()

    lane_row = lax.broadcasted_iota(jnp.int32, (1, two), 1) % rows
    key_pos = y * (2 * klen) + lax.broadcasted_iota(jnp.int32, (2 * klen, two), 0)
    offset = off_ref[0]
    stat_row = lax.broadcasted_iota(jnp.int32, (16, HD), 0)
    scale = HD ** (-0.5) * LOG2E

    for d in (0, 1):
        for h in (0, 1):
            rcv[d, 0, h, 0:HD, :] = jnp.zeros((HD, HD), BF)
            rcv[d, 0, h, HD:, :] = jnp.where(stat_row == 0, NEG, 0.0).astype(BF)

    for slot in range(AHEAD):
        for d in (0, 1):
            q_arrival(d, slot).wait_recv()
            q_hop(d, slot).start()
    for c in local_q:
        c.wait()
    local_k.wait()
    local_v.wait()
    send_k.wait_recv()
    send_v.wait_recv()
    vt[...] = vbuf[...].T

    def acc_hop(d, t, h):
        return remote(snd.at[d, t, h], rcv.at[d, t + 1, h], a_s.at[d, t, h], a_r.at[d, t + 1, h], ring[d])

    def acc_arrival(d, t, h):
        return remote(snd.at[d, t, h], rcv.at[d, t, h], a_s.at[d, t, h], a_r.at[d, t, h], ring[d])

    def advance(t, carry):
        for d in (0, 1):
            ahead = t + AHEAD

            @pl.when(ahead < ny - 1)
            def _():
                q_arrival(d, ahead).wait_recv()

            @pl.when(ahead < ny - 2)
            def _():
                q_hop(d, ahead).start()

        for d in (0, 1):
            block = (y + 2 * ny - 1 - t) % ny if d == 0 else (y + 1 + t) % ny
            q2 = qb[d, t]
            q2 = jnp.concatenate([q2[:, :HD], q2[:, HD:]], axis=0)
            scores = lax.dot_general(
                kbuf[...], q2, (((1,), (1,)), ((), ())), preferred_element_type=F32
            )
            row_pos = offset + (block * 2 + zl) * rows + lane_row
            scores = jnp.where(key_pos <= row_pos, scores, NEG)
            top = jnp.max(scores, axis=0, keepdims=True).astype(BF).astype(F32)
            weights = jnp.exp2((scores - top) * scale)
            total = jnp.sum(weights, axis=0, keepdims=True)
            mixed = jnp.dot(vt[...], weights.astype(BF), preferred_element_type=F32)
            for h in (0, 1):
                cols = slice(h * HD, (h + 1) * HD)

                @pl.when(t > 0)
                def _():
                    acc_arrival(d, t, h).wait_recv()

                stats = rcv[d, t, h, HD:, :].astype(F32)
                top_in = stats[0:1]
                sum_in = stats[1:2] + stats[2:3]
                top_new = jnp.maximum(top_in, top[:, cols])
                f_in = jnp.exp2((top_in - top_new) * scale)
                f_own = jnp.exp2((top[:, cols] - top_new) * scale)
                sum_new = sum_in * f_in + total[:, cols] * f_own
                acc_new = rcv[d, t, h, 0:HD, :].astype(F32) * f_in + mixed[:, cols] * f_own

                @pl.when(t < ny - 1)
                def _():
                    snd[d, t, h, 0:HD, :] = acc_new.astype(BF)
                    high = sum_new.astype(BF).astype(F32)
                    packed = jnp.where(
                        stat_row == 0,
                        top_new,
                        jnp.where(stat_row == 1, high, jnp.where(stat_row == 2, sum_new - high, 0.0)),
                    )
                    snd[d, t, h, HD:, :] = packed.astype(BF)
                    acc_hop(d, t, h).start()

                @pl.when(t == ny - 1)
                def _():
                    head = (acc_new / sum_new).T
                    att[co, :, (2 * d + h) * HD : (2 * d + h + 1) * HD] = head.astype(BF)

        return carry

    lax.fori_loop(0, ny, advance, 0)

    send_t = remote(att.at[co], att.at[co], t_s, t_r, core_mate)
    send_t.start()
    for c in local_w:
        c.wait()
    for c in send_w:
        c.wait_recv()
    send_t.wait_recv()

    def product(away):
        dest = (zh + away) % nzh
        out = jnp.dot(att[0], wbuf[dest, 0], preferred_element_type=F32)
        return out + jnp.dot(att[1], wbuf[dest, 1], preferred_element_type=F32)

    def span(i, j):
        return slice(i * half + j * part, i * half + (j + 1) * part)

    far_cp = [[remote(far_s.at[i, j], far_r.at[i, j], far_ss.at[i, j], far_rs.at[i, j], zring[i]) for j in range(PARTS)] for i in (0, 1)]
    near_cp = [[remote(near_s.at[i, j], near_r.at[i, j], near_ss.at[i, j], near_rs.at[i, j], zring[i]) for j in range(PARTS)] for i in (0, 1)]
    mix_cp = [[remote(mix_s.at[i, j], mix_r.at[i, j], mix_ss.at[i, j], mix_rs.at[i, j], zring[i]) for j in range(PARTS)] for i in (0, 1)]
    fin_cp = [
        [remote(fin.at[span(i, j)], o_ref.at[span(i, j)], x_s.at[i, j], x_r.at[i, j], x_next) for j in range(PARTS)]
        for i in (0, 1)
    ]

    opposite = product(2)
    for j in range(PARTS):
        for i in (0, 1):
            far_s[i, j] = opposite[span(i, j)].astype(BF)
            far_cp[i][j].start()
    for i in (0, 1):
        out = product(1 if i == 0 else nzh - 1)
        keep[i] = out[i * half : (i + 1) * half]
        for j in range(PARTS):
            near_s[i, j] = out[span(1 - i, j)].astype(BF)
            near_cp[i][j].start()
    base[...] = product(0) + res_ref[...].astype(F32)
    for j in range(PARTS):
        for i in (0, 1):
            far_cp[i][j].wait_recv()
            mix_s[i, j] = (keep[i, j * part : (j + 1) * part] + far_r[i, j].astype(F32)).astype(BF)
            mix_cp[i][j].start()
    for j in range(PARTS):
        for i in (0, 1):
            near_cp[1 - i][j].wait_recv()
            mix_cp[i][j].wait_recv()
            summed = base[span(i, j)] + near_r[1 - i, j].astype(F32) + mix_r[i, j].astype(F32)
            fin[span(i, j)] = summed.astype(BF)
            fin_cp[i][j].start()

    send_k.wait_send()
    send_v.wait_send()
    for c in send_w:
        c.wait_send()
    send_t.wait_send()

    def drain_q(s, carry):
        for d in (0, 1):
            q_arrival(d, s).wait_send()
            for h in (0, 1):
                acc_hop(d, s, h).wait_send()
        return carry

    lax.fori_loop(0, ny - 1, drain_q, 0)
    for i in (0, 1):
        for j in range(PARTS):
            far_cp[i][j].wait_send()
            near_cp[i][j].wait_send()
            mix_cp[i][j].wait_send()
    for i in (0, 1):
        for j in range(PARTS):
            fin_cp[i][j].wait_send()
            fin_cp[i][j].wait_recv()


def on_device(ny, nzh, nx, row_offsets, queries, cache_keys, cache_values, residual, out_weight):
    q, k, v, res, w = queries[0], cache_keys[0], cache_values[0], residual[0], out_weight[0]
    rows, klen, width = q.shape[0], k.shape[0], res.shape[1]
    half = rows // 2
    part = half // PARTS
    dma = pltpu.SemaphoreType.DMA
    piece = pltpu.VMEM((2, PARTS, part, width), BF)
    any_spec = pl.BlockSpec(memory_space=pl.ANY)
    out = pl.pallas_call(
        functools.partial(kernel, ny, nzh, nx),
        out_shape=jax.ShapeDtypeStruct(res.shape, BF),
        in_specs=[
            pl.BlockSpec(memory_space=pltpu.SMEM),
            any_spec, any_spec, any_spec,
            pl.BlockSpec(memory_space=pltpu.VMEM),
            any_spec,
        ],
        out_specs=any_spec,
        scratch_shapes=[
            pltpu.VMEM((2 * klen, HD), BF),
            pltpu.VMEM((2 * klen, HD), BF),
            pltpu.VMEM((HD, 2 * klen), BF),
            pltpu.VMEM((2, ny, rows, 2 * HD), BF),
            pltpu.VMEM((2, ny, 2, HD + 16, HD), BF),
            pltpu.VMEM((2, ny, 2, HD + 16, HD), BF),
            pltpu.VMEM((2, rows, G * HD), BF),
            pltpu.VMEM((nzh, 2, w.shape[0], width), BF),
            pltpu.VMEM((2, half, width), F32),
            pltpu.VMEM((rows, width), F32),
            piece, piece, piece, piece, piece, piece,
            pltpu.VMEM((rows, width), BF),
            dma((2,)), dma((2,)), dma((2,)),
            dma((2,)), dma((2, ny)), dma((2, ny)),
            dma((2, ny, 2)), dma((2, ny, 2)),
            dma((nzh,)), dma((nzh,)), dma((nzh,)),
            dma(()), dma(()),
            dma((2, PARTS)), dma((2, PARTS)), dma((2, PARTS)), dma((2, PARTS)), dma((2, PARTS)), dma((2, PARTS)),
            dma((2, PARTS)), dma((2, PARTS)),
        ],
        compiler_params=pltpu.CompilerParams(
            collective_id=0, has_side_effects=True, vmem_limit_bytes=48 * 1024 * 1024
        ),
    )(row_offsets, q, k, v, res, w)
    return out[None]


def solution(mesh):
    placed = (
        P("section"),
        P("section", "ctx", "tp"),
        P("section", "ctx", "tp"),
        P("section", "ctx", "tp"),
        P("section", "ctx", "tp"),
        P("section", "tp", None),
    )
    ny, nzh, nx = mesh.shape["ctx"] // 2, mesh.shape["tp"] // 2, mesh.shape["section"]
    return jax.shard_map(
        functools.partial(on_device, ny, nzh, nx),
        mesh=mesh, in_specs=placed, out_specs=P("section", "ctx", "tp"), check_vma=False,
    )
```

```python
import functools

import jax
import jax.numpy as jnp
from jax import lax
from jax.experimental import pallas as pl
from jax.experimental.pallas import tpu as pltpu
from jax.sharding import PartitionSpec as P

HD = 128
G = 4
NEG = -(2.0**100)
LOG2E = 1.4426950408889634
PARTS = 2
MESH = pl.DeviceIdType.MESH
BF = jnp.bfloat16
F32 = jnp.float32


def kernel(
    ny, nzh, nx,
    off_ref, q_ref, k_ref, v_ref, res_ref, w_ref, o_ref,
    kb, vb, qin, qs, m_ref, l_ref, acc, snd, rcv, att, wbuf, resv, keep, base,
    far_s, far_r, near_s, near_r, mix_s, mix_r, fin,
    loc, kv_s, kv_r, q_s, q_r, a_s, a_r, w_l, w_s, w_r, t_s, t_r,
    far_ss, far_rs, near_ss, near_rs, mix_ss, mix_rs, x_s, x_r,
):
    rows = q_ref.shape[0]
    klen = k_ref.shape[0]
    width = res_ref.shape[1]
    half = rows // 2
    part = half // PARTS
    two = 2 * HD
    hops = ny // 2
    cut = (klen // HD + 1) // 2 * HD
    spans = ((0, cut), (cut, klen - cut))

    ctx = lax.axis_index("ctx")
    tp = lax.axis_index("tp")
    x = lax.axis_index("section")
    y, zl = ctx // 2, ctx % 2
    zh, co = tp // 2, tp % 2
    y_next = {"ctx": ((y + 1) % ny) * 2 + zl}
    y_prev = {"ctx": ((y + ny - 1) % ny) * 2 + zl}
    ring = (y_next, y_prev)
    z_mate = {"ctx": y * 2 + 1 - zl}
    core_mate = {"tp": zh * 2 + 1 - co}
    zh_next = {"tp": ((zh + 1) % nzh) * 2 + co}
    zh_prev = {"tp": ((zh + nzh - 1) % nzh) * 2 + co}
    zring = (zh_next, zh_prev)
    x_next = {"section": (x + 1) % nx}
    x_prev = {"section": (x + nx - 1) % nx}

    def remote(src, dst, s, r, where):
        return pltpu.make_async_remote_copy(
            src_ref=src, dst_ref=dst, send_sem=s, recv_sem=r, device_id=where, device_id_type=MESH
        )

    def wcols(block, core):
        return pl.ds(pl.multiple_of(block * 2 * width + core * width, width), width)

    local_k = pltpu.make_async_copy(k_ref, kb.at[0], loc.at[0])
    local_v = pltpu.make_async_copy(v_ref, vb.at[0], loc.at[1])
    local_q = pltpu.make_async_copy(q_ref, qin.at[0], loc.at[2])
    local_r = pltpu.make_async_copy(res_ref, resv, loc.at[3])
    local_w = [
        pltpu.make_async_copy(w_ref.at[:, wcols(b, co)], wbuf.at[b, co], w_l.at[b]) for b in range(nzh)
    ]
    local_q.start()
    local_k.start()
    local_v.start()

    barrier = pltpu.get_barrier_semaphore()
    greet = (y_next, y_prev, z_mate, core_mate, zh_next, zh_prev, x_next, x_prev)
    for where in greet:
        pl.semaphore_signal(barrier, inc=1, device_id=where, device_id_type=MESH)
    pl.semaphore_wait(barrier, len(greet))

    def hop(src, slot, i, way, kind):
        at = pl.ds(*spans[i])
        dst = (kb, vb)[kind].at[slot, at]
        return remote(src.at[at], dst, kv_s.at[slot, i, kind], kv_r.at[slot, i, kind], ring[way])

    send_q = remote(q_ref, qin.at[1], q_s, q_r, z_mate)
    for i in (0, 1):
        for kind in (0, 1):
            for way in (0, 1):
                hop((k_ref, v_ref)[kind], 1 + way, i, way, kind).start()
        if i == 0:
            send_q.start()
    send_w = [
        remote(w_ref.at[:, wcols(b, 1 - co)], wbuf.at[b, co], w_s.at[b], w_r.at[b], core_mate)
        for b in range(nzh)
    ]
    for c in send_w:
        c.start()
    for c in local_w:
        c.start()
    local_r.start()

    m_ref[...] = jnp.full(m_ref.shape, NEG, F32)
    l_ref[...] = jnp.zeros(l_ref.shape, F32)
    acc[...] = jnp.zeros(acc.shape, F32)
    lane_row = lax.broadcasted_iota(jnp.int32, (1, two), 1) % rows
    offset = off_ref[0]
    stat_row = lax.broadcasted_iota(jnp.int32, (16, two), 0)
    scale = HD ** (-0.5) * LOG2E

    def lay_queries(c):
        for g in (0, 1):
            for h in (0, 1):
                col = (2 * g + h) * HD
                qs[2 * c + g, h * rows : (h + 1) * rows, :] = qin[c, :, col : col + HD]

    def attend(slot, block, i, first, last):
        start, size = spans[i]

        def group(g, carry):
            other = g // 2
            row_pos = offset + (y * 2 + zl + other * (1 - 2 * zl)) * rows + lane_row
            key_pos = (block * 2 + zl) * klen + start + lax.broadcasted_iota(jnp.int32, (size, two), 0)
            scores = lax.dot_general(
                kb[slot, start : start + size, :],
                qs[g],
                (((1,), (1,)), ((), ())),
                preferred_element_type=F32,
            )
            scores = jnp.where(key_pos <= row_pos, scores, NEG)
            top = jnp.max(scores, axis=0, keepdims=True).astype(BF).astype(F32)
            top_old = m_ref[g]
            top = jnp.maximum(top, top_old)
            weights = jnp.exp2((scores - top) * scale)
            fade = jnp.exp2((top_old - top) * scale)
            m_ref[g] = top
            l_ref[g] = l_ref[g] * fade + jnp.sum(weights, axis=0, keepdims=True)
            mixed = lax.dot_general(
                vb[slot, start : start + size, :],
                weights.astype(BF),
                (((0,), (0,)), ((), ())),
                preferred_element_type=F32,
            )
            acc[g] = acc[g] * fade + mixed
            return carry

        lax.fori_loop(first, last, group, 0)

    def arrive(slot, i, way, kind):
        return hop((kb, vb)[kind].at[slot], slot, i, way, kind)

    local_q.wait()
    lay_queries(0)
    local_k.wait()
    local_v.wait()
    for i in (0, 1):
        attend(0, y, i, 0, 2)

    def round_trip(h, carry):
        for i in (0, 1):
            for kind in (0, 1):
                for way in (0, 1):
                    slot = 2 * h - 1 + way
                    arrive(slot, i, way, kind).wait_recv()
                    dest = 2 * h + 1 if way == 0 else jnp.minimum(2 * h + 2, ny - 1)
                    onward = hop((kb, vb)[kind].at[slot], dest, i, way, kind)
                    if way == i:
                        onward.start()
                    else:

                        @pl.when(h < hops - 1)
                        def _():
                            onward.start()

            if i == 0:

                @pl.when(h == 1)
                def _():
                    send_q.wait_recv()
                    lay_queries(1)
                    for j in (0, 1):
                        attend(0, y, j, 2, 4)

            def each(way, c):
                block = (y + ny + way * 2 * h - h) % ny
                attend(2 * h - 1 + way, block, i, 0, 4)
                return c

            lax.fori_loop(0, 2, each, 0)
        return carry

    lax.fori_loop(1, hops, round_trip, 0)

    last = ny - 1
    far_block = (y + hops) % ny
    for kind in (0, 1):
        arrive(last, 0, 0, kind).wait_recv()
    attend(last, far_block, 0, 0, 4)
    for kind in (0, 1):
        arrive(last, 1, 1, kind).wait_recv()
    attend(last, far_block, 1, 2, 4)
    send_a = [remote(snd.at[g], rcv.at[g], a_s.at[g], a_r.at[g], z_mate) for g in (0, 1)]
    for g in (0, 1):
        snd[g, 0:HD, :] = acc[2 + g].astype(BF)
        total = l_ref[2 + g]
        high = total.astype(BF).astype(F32)
        packed = jnp.where(
            stat_row == 0,
            m_ref[2 + g],
            jnp.where(stat_row == 1, high, jnp.where(stat_row == 2, total - high, 0.0)),
        )
        snd[g, HD:, :] = packed.astype(BF)
        send_a[g].start()
    attend(last, far_block, 1, 0, 2)
    for g in (0, 1):
        send_a[g].wait_recv()
        stats = rcv[g, HD:, :].astype(F32)
        top_in = stats[0:1]
        sum_in = stats[1:2] + stats[2:3]
        top_new = jnp.maximum(top_in, m_ref[g])
        f_in = jnp.exp2((top_in - top_new) * scale)
        f_own = jnp.exp2((m_ref[g] - top_new) * scale)
        sum_new = sum_in * f_in + l_ref[g] * f_own
        head = (rcv[g, 0:HD, :].astype(F32) * f_in + acc[g] * f_own) / sum_new
        for h in (0, 1):
            col = (2 * g + h) * HD
            att[co, :, col : col + HD] = head[:, h * rows : (h + 1) * rows].T.astype(BF)

    send_t = remote(att.at[co], att.at[co], t_s, t_r, core_mate)
    send_t.start()
    for c in local_w:
        c.wait()
    for c in send_w:
        c.wait_recv()
    local_r.wait()
    send_t.wait_recv()

    def product(away):
        dest = (zh + away) % nzh
        out = jnp.dot(att[0], wbuf[dest, 0], preferred_element_type=F32)
        return out + jnp.dot(att[1], wbuf[dest, 1], preferred_element_type=F32)

    def span(i, j):
        return slice(i * half + j * part, i * half + (j + 1) * part)

    far_cp = [[remote(far_s.at[i, j], far_r.at[i, j], far_ss.at[i, j], far_rs.at[i, j], zring[i]) for j in range(PARTS)] for i in (0, 1)]
    near_cp = [[remote(near_s.at[i, j], near_r.at[i, j], near_ss.at[i, j], near_rs.at[i, j], zring[i]) for j in range(PARTS)] for i in (0, 1)]
    mix_cp = [[remote(mix_s.at[i, j], mix_r.at[i, j], mix_ss.at[i, j], mix_rs.at[i, j], zring[i]) for j in range(PARTS)] for i in (0, 1)]
    fin_cp = [
        [remote(fin.at[span(i, j)], o_ref.at[span(i, j)], x_s.at[i, j], x_r.at[i, j], x_next) for j in range(PARTS)]
        for i in (0, 1)
    ]

    opposite = product(2)
    for j in range(PARTS):
        for i in (0, 1):
            far_s[i, j] = opposite[span(i, j)].astype(BF)
            far_cp[i][j].start()
    for i in (0, 1):
        out = product(1 if i == 0 else nzh - 1)
        keep[i] = out[i * half : (i + 1) * half]
        for j in range(PARTS):
            near_s[i, j] = out[span(1 - i, j)].astype(BF)
            near_cp[i][j].start()
    base[...] = product(0) + resv[...].astype(F32)
    for j in range(PARTS):
        for i in (0, 1):
            far_cp[i][j].wait_recv()
            mix_s[i, j] = (keep[i, j * part : (j + 1) * part] + far_r[i, j].astype(F32)).astype(BF)
            mix_cp[i][j].start()
    for j in range(PARTS):
        for i in (0, 1):
            near_cp[1 - i][j].wait_recv()
            mix_cp[i][j].wait_recv()
            summed = base[span(i, j)] + near_r[1 - i, j].astype(F32) + mix_r[i, j].astype(F32)
            fin[span(i, j)] = summed.astype(BF)
            fin_cp[i][j].start()

    send_q.wait_send()
    for c in send_w:
        c.wait_send()
    send_t.wait_send()
    for c in send_a:
        c.wait_send()

    def drain(slot, carry):
        for i in (0, 1):
            for kind in (0, 1):
                arrive(slot, i, 0, kind).wait_send()
        return carry

    lax.fori_loop(1, ny, drain, 0)
    for i in (0, 1):
        for j in range(PARTS):
            far_cp[i][j].wait_send()
            near_cp[i][j].wait_send()
            mix_cp[i][j].wait_send()
    for i in (0, 1):
        for j in range(PARTS):
            fin_cp[i][j].wait_send()
            fin_cp[i][j].wait_recv()


def on_device(ny, nzh, nx, row_offsets, queries, cache_keys, cache_values, residual, out_weight):
    q, k, v, res, w = queries[0], cache_keys[0], cache_values[0], residual[0], out_weight[0]
    rows, klen, width = q.shape[0], k.shape[0], res.shape[1]
    half = rows // 2
    part = half // PARTS
    dma = pltpu.SemaphoreType.DMA
    piece = pltpu.VMEM((2, PARTS, part, width), BF)
    any_spec = pl.BlockSpec(memory_space=pl.ANY)
    out = pl.pallas_call(
        functools.partial(kernel, ny, nzh, nx),
        out_shape=jax.ShapeDtypeStruct(res.shape, BF),
        in_specs=[pl.BlockSpec(memory_space=pltpu.SMEM)] + [any_spec] * 5,
        out_specs=any_spec,
        scratch_shapes=[
            pltpu.VMEM((ny, klen, HD), BF),
            pltpu.VMEM((ny, klen, HD), BF),
            pltpu.VMEM((2, rows, G * HD), BF),
            pltpu.VMEM((4, 2 * rows, HD), BF),
            pltpu.VMEM((4, 1, 2 * HD), F32),
            pltpu.VMEM((4, 1, 2 * HD), F32),
            pltpu.VMEM((4, HD, 2 * HD), F32),
            pltpu.VMEM((2, HD + 16, 2 * HD), BF),
            pltpu.VMEM((2, HD + 16, 2 * HD), BF),
            pltpu.VMEM((2, rows, G * HD), BF),
            pltpu.VMEM((nzh, 2, w.shape[0], width), BF),
            pltpu.VMEM((rows, width), BF),
            pltpu.VMEM((2, half, width), F32),
            pltpu.VMEM((rows, width), F32),
            piece, piece, piece, piece, piece, piece,
            pltpu.VMEM((rows, width), BF),
            dma((4,)), dma((ny, 2, 2)), dma((ny, 2, 2)),
            dma(()), dma(()), dma((2,)), dma((2,)),
            dma((nzh,)), dma((nzh,)), dma((nzh,)),
            dma(()), dma(()),
            dma((2, PARTS)), dma((2, PARTS)), dma((2, PARTS)), dma((2, PARTS)), dma((2, PARTS)), dma((2, PARTS)),
            dma((2, PARTS)), dma((2, PARTS)),
        ],
        compiler_params=pltpu.CompilerParams(
            collective_id=0, has_side_effects=True, vmem_limit_bytes=64 * 1024 * 1024 - 70000
        ),
    )(row_offsets, q, k, v, res, w)
    return out[None]


def solution(mesh):
    placed = (
        P("section"),
        P("section", "ctx", "tp"),
        P("section", "ctx", "tp"),
        P("section", "ctx", "tp"),
        P("section", "ctx", "tp"),
        P("section", "tp", None),
    )
    ny, nzh, nx = mesh.shape["ctx"] // 2, mesh.shape["tp"] // 2, mesh.shape["section"]
    return jax.shard_map(
        functools.partial(on_device, ny, nzh, nx),
        mesh=mesh, in_specs=placed, out_specs=P("section", "ctx", "tp"), check_vma=False,
    )
```

```python
import functools

import jax
import jax.numpy as jnp
from jax import lax
from jax.experimental import pallas as pl
from jax.experimental.pallas import tpu as pltpu
from jax.sharding import PartitionSpec as P

HD = 128
G = 4
NEG = -(2.0**100)
LOG2E = 1.4426950408889634
PARTS = 2
MESH = pl.DeviceIdType.MESH
BF = jnp.bfloat16
F32 = jnp.float32


def kernel(
    ny, nzh, nx,
    off_ref, q_ref, k_ref, v_ref, res_ref, w_ref, o_ref,
    kb, vb, vt, qin, qs, m_ref, l_ref, acc, snd, rcv, att, wbuf, resv, keep,
    far_s, far_r, near_s, near_r, mix_s, mix_r, own_s, own_r, fin,
    loc, kv_s, kv_r, q_s, q_r, a_s, a_r, w_l, w_s, w_r, t_s, t_r,
    far_ss, far_rs, near_ss, near_rs, mix_ss, mix_rs, own_ss, own_rs, r_s, r_r, o_l,
):
    rows = q_ref.shape[0]
    klen = k_ref.shape[0]
    width = res_ref.shape[1]
    half = rows // 2
    part = half // PARTS
    two = 2 * HD
    hops = ny // 2
    cut = (klen // HD + 1) // 2 * HD
    spans = ((0, cut), (cut, klen - cut))

    ctx = lax.axis_index("ctx")
    tp = lax.axis_index("tp")
    x = lax.axis_index("section")
    y, zl = ctx // 2, ctx % 2
    zh, co = tp // 2, tp % 2
    y_next = {"ctx": ((y + 1) % ny) * 2 + zl}
    y_prev = {"ctx": ((y + ny - 1) % ny) * 2 + zl}
    ring = (y_next, y_prev)
    z_mate = {"ctx": y * 2 + 1 - zl}
    core_mate = {"tp": zh * 2 + 1 - co}
    zh_next = {"tp": ((zh + 1) % nzh) * 2 + co}
    zh_prev = {"tp": ((zh + nzh - 1) % nzh) * 2 + co}
    zring = (zh_next, zh_prev)
    x_next = {"section": (x + 1) % nx}
    x_prev = {"section": (x + nx - 1) % nx}
    landing = tuple({**x_next, **z} for z in zring)
    leaving = tuple({**x_prev, **z} for z in zring)

    def remote(src, dst, s, r, where):
        return pltpu.make_async_remote_copy(
            src_ref=src, dst_ref=dst, send_sem=s, recv_sem=r, device_id=where, device_id_type=MESH
        )

    def wcols(block, core):
        return pl.ds(pl.multiple_of(block * 2 * width + core * width, width), width)

    local_k = pltpu.make_async_copy(k_ref, kb.at[0], loc.at[0])
    local_v = pltpu.make_async_copy(v_ref, vb.at[0], loc.at[1])
    local_q = pltpu.make_async_copy(q_ref, qin.at[0], loc.at[2])
    local_w = [
        pltpu.make_async_copy(w_ref.at[:, wcols(b, co)], wbuf.at[b, co], w_l.at[b]) for b in range(nzh)
    ]
    local_q.start()
    local_k.start()
    local_v.start()

    barrier = pltpu.get_barrier_semaphore()
    greet = (y_next, y_prev, z_mate, core_mate, zh_next, zh_prev, x_next, x_prev) + landing + leaving
    for where in greet:
        pl.semaphore_signal(barrier, inc=1, device_id=where, device_id_type=MESH)
    pl.semaphore_wait(barrier, len(greet))

    def hop(src, slot, i, way, kind):
        at = pl.ds(*spans[i])
        dst = (kb, vb)[kind].at[slot, at]
        return remote(src.at[at], dst, kv_s.at[slot, i, kind], kv_r.at[slot, i, kind], ring[way])

    send_q = remote(q_ref, qin.at[1], q_s, q_r, z_mate)
    for i in (0, 1):
        for kind in (0, 1):
            for way in (0, 1):
                hop((k_ref, v_ref)[kind], 1 + way, i, way, kind).start()
        if i == 0:
            send_q.start()
    send_w = [
        remote(w_ref.at[:, wcols(b, 1 - co)], wbuf.at[b, co], w_s.at[b], w_r.at[b], core_mate)
        for b in range(nzh)
    ]
    for c in send_w:
        c.start()
    for c in local_w:
        c.start()
    send_r = remote(res_ref, resv, r_s, r_r, x_next)
    send_r.start()

    m_ref[...] = jnp.full(m_ref.shape, NEG, F32)
    l_ref[...] = jnp.zeros(l_ref.shape, F32)
    acc[...] = jnp.zeros(acc.shape, F32)
    lane_row = lax.broadcasted_iota(jnp.int32, (1, two), 1) % rows
    offset = off_ref[0]
    stat_row = lax.broadcasted_iota(jnp.int32, (16, two), 0)
    scale = HD ** (-0.5) * LOG2E

    def lay_queries(c):
        for g in (0, 1):
            for h in (0, 1):
                col = (2 * g + h) * HD
                qs[2 * c + g, h * rows : (h + 1) * rows, :] = qin[c, :, col : col + HD]

    def turn(slot, start, size):
        vt[slot, :, start : start + size] = vb[slot, start : start + size, :].T

    def attend(slot, block, start, size, first, last):
        key_pos = (block * 2 + zl) * klen + start + lax.broadcasted_iota(jnp.int32, (size, two), 0)

        def row_class(other, carry):
            row_pos = offset + (y * 2 + zl + other * (1 - 2 * zl)) * rows + lane_row
            visible = key_pos <= row_pos
            for g in (2 * other, 2 * other + 1):
                scores = lax.dot_general(
                    kb[slot, start : start + size, :], qs[g], (((1,), (1,)), ((), ())), preferred_element_type=F32
                )
                scores = jnp.where(visible, scores, NEG)
                top_old = m_ref[g]
                top = jnp.maximum(jnp.max(scores, axis=0, keepdims=True).astype(BF).astype(F32), top_old)
                weights = jnp.exp2((scores - top) * scale)
                fade = jnp.exp2((top_old - top) * scale)
                m_ref[g] = top
                l_ref[g] = l_ref[g] * fade + jnp.sum(weights, axis=0, keepdims=True)
                mixed = jnp.dot(
                    vt[slot, :, start : start + size], weights.astype(BF), preferred_element_type=F32
                )
                acc[g] = acc[g] * fade + mixed
            return carry

        lax.fori_loop(first, last, row_class, 0)

    def arrive(slot, i, way, kind):
        return hop((kb, vb)[kind].at[slot], slot, i, way, kind)

    local_q.wait()
    lay_queries(0)
    local_k.wait()
    local_v.wait()
    turn(0, 0, klen)
    attend(0, y, 0, klen, 0, 1)

    def forward(h, i):
        for kind in (0, 1):
            for way in (0, 1):
                slot = 2 * h - 1 + way
                arrive(slot, i, way, kind).wait_recv()
                dest = 2 * h + 1 if way == 0 else jnp.minimum(2 * h + 2, ny - 1)
                onward = hop((kb, vb)[kind].at[slot], dest, i, way, kind)
                if way == i:
                    onward.start()
                else:

                    @pl.when(h < hops - 1)
                    def _():
                        onward.start()

    def round_trip(h, carry):
        forward(h, 0)

        @pl.when(h == 1)
        def _():
            send_q.wait_recv()
            lay_queries(1)
            attend(0, y, 0, klen, 1, 2)

        @pl.when(h > 1)
        def _():
            turn(2 * h - 2, 0, klen)
            attend(2 * h - 2, (y + h - 1) % ny, 0, klen, 0, 2)

        forward(h, 1)
        turn(2 * h - 1, 0, klen)
        attend(2 * h - 1, (y + ny - h) % ny, 0, klen, 0, 2)
        return carry

    lax.fori_loop(1, hops, round_trip, 0)

    last = ny - 1
    far_block = (y + hops) % ny
    for kind in (0, 1):
        arrive(last, 0, 0, kind).wait_recv()
    turn(last - 1, 0, klen)
    attend(last - 1, (y + hops - 1) % ny, 0, klen, 0, 2)
    turn(last, 0, cut)
    attend(last, far_block, 0, cut, 0, 2)
    for kind in (0, 1):
        arrive(last, 1, 1, kind).wait_recv()
    turn(last, cut, klen - cut)
    attend(last, far_block, cut, klen - cut, 1, 2)
    send_a = [remote(snd.at[g], rcv.at[g], a_s.at[g], a_r.at[g], z_mate) for g in (0, 1)]
    for g in (0, 1):
        snd[g, 0:HD, :] = acc[2 + g].astype(BF)
        total = l_ref[2 + g]
        high = total.astype(BF).astype(F32)
        packed = jnp.where(
            stat_row == 0,
            m_ref[2 + g],
            jnp.where(stat_row == 1, high, jnp.where(stat_row == 2, total - high, 0.0)),
        )
        snd[g, HD:, :] = packed.astype(BF)
        send_a[g].start()
    attend(last, far_block, cut, klen - cut, 0, 1)
    for g in (0, 1):
        send_a[g].wait_recv()
        stats = rcv[g, HD:, :].astype(F32)
        top_in = stats[0:1]
        sum_in = stats[1:2] + stats[2:3]
        top_new = jnp.maximum(top_in, m_ref[g])
        f_in = jnp.exp2((top_in - top_new) * scale)
        f_own = jnp.exp2((m_ref[g] - top_new) * scale)
        sum_new = sum_in * f_in + l_ref[g] * f_own
        head = (rcv[g, 0:HD, :].astype(F32) * f_in + acc[g] * f_own) / sum_new
        for h in (0, 1):
            col = (2 * g + h) * HD
            att[co, :, col : col + HD] = head[:, h * rows : (h + 1) * rows].T.astype(BF)

    send_t = remote(att.at[co], att.at[co], t_s, t_r, core_mate)
    send_t.start()
    for c in local_w:
        c.wait()
    for c in send_w:
        c.wait_recv()
    send_t.wait_recv()

    def product(away):
        dest = (zh + away) % nzh
        out = jnp.dot(att[0], wbuf[dest, 0], preferred_element_type=F32)
        return out + jnp.dot(att[1], wbuf[dest, 1], preferred_element_type=F32)

    def span(i, j):
        return slice(i * half + j * part, i * half + (j + 1) * part)

    far_cp = [[remote(far_s.at[i, j], far_r.at[i, j], far_ss.at[i, j], far_rs.at[i, j], zring[i]) for j in range(PARTS)] for i in (0, 1)]
    near_cp = [[remote(near_s.at[i, j], near_r.at[i, j], near_ss.at[i, j], near_rs.at[i, j], landing[i]) for j in range(PARTS)] for i in (0, 1)]
    mix_cp = [[remote(mix_s.at[i, j], mix_r.at[i, j], mix_ss.at[i, j], mix_rs.at[i, j], landing[i]) for j in range(PARTS)] for i in (0, 1)]
    own_cp = [[remote(own_s.at[i, j], own_r.at[i, j], own_ss.at[i, j], own_rs.at[i, j], x_next) for j in range(PARTS)] for i in (0, 1)]
    out_cp = [[pltpu.make_async_copy(fin.at[span(i, j)], o_ref.at[span(i, j)], o_l.at[i, j]) for j in range(PARTS)] for i in (0, 1)]

    opposite = product(2)
    for j in range(PARTS):
        for i in (0, 1):
            far_s[i, j] = opposite[span(i, j)].astype(BF)
            far_cp[i][j].start()
    own = product(0)
    for j in range(PARTS):
        for i in (0, 1):
            own_s[i, j] = own[span(i, j)].astype(BF)
            own_cp[i][j].start()
    for i in (0, 1):
        out = product(1 if i == 0 else nzh - 1)
        keep[i] = out[i * half : (i + 1) * half]
        for j in range(PARTS):
            near_s[i, j] = out[span(1 - i, j)].astype(BF)
            near_cp[i][j].start()
    for j in range(PARTS):
        for i in (0, 1):
            far_cp[i][j].wait_recv()
            mix_s[i, j] = (keep[i, j * part : (j + 1) * part] + far_r[i, j].astype(F32)).astype(BF)
            mix_cp[i][j].start()
    send_r.wait_recv()
    for j in range(PARTS):
        for i in (0, 1):
            own_cp[i][j].wait_recv()
            near_cp[1 - i][j].wait_recv()
            mix_cp[i][j].wait_recv()
            summed = own_r[i, j].astype(F32) + near_r[1 - i, j].astype(F32) + mix_r[i, j].astype(F32)
            fin[span(i, j)] = (resv[span(i, j)].astype(F32) + summed).astype(BF)
            out_cp[i][j].start()

    send_q.wait_send()
    send_r.wait_send()
    for c in send_w:
        c.wait_send()
    send_t.wait_send()
    for c in send_a:
        c.wait_send()

    def drain(slot, carry):
        for i in (0, 1):
            for kind in (0, 1):
                arrive(slot, i, 0, kind).wait_send()
        return carry

    lax.fori_loop(1, ny, drain, 0)
    for i in (0, 1):
        for j in range(PARTS):
            far_cp[i][j].wait_send()
            own_cp[i][j].wait_send()
            near_cp[i][j].wait_send()
            mix_cp[i][j].wait_send()
            out_cp[i][j].wait()


def on_device(ny, nzh, nx, row_offsets, queries, cache_keys, cache_values, residual, out_weight):
    q, k, v, res, w = queries[0], cache_keys[0], cache_values[0], residual[0], out_weight[0]
    rows, klen, width = q.shape[0], k.shape[0], res.shape[1]
    half = rows // 2
    part = half // PARTS
    dma = pltpu.SemaphoreType.DMA
    piece = pltpu.VMEM((2, PARTS, part, width), BF)
    any_spec = pl.BlockSpec(memory_space=pl.ANY)
    out = pl.pallas_call(
        functools.partial(kernel, ny, nzh, nx),
        out_shape=jax.ShapeDtypeStruct(res.shape, BF),
        in_specs=[pl.BlockSpec(memory_space=pltpu.SMEM)] + [any_spec] * 5,
        out_specs=any_spec,
        scratch_shapes=[
            pltpu.VMEM((ny, klen, HD), BF),
            pltpu.VMEM((ny, klen, HD), BF),
            pltpu.VMEM((ny, HD, klen), BF),
            pltpu.VMEM((2, rows, G * HD), BF),
            pltpu.VMEM((4, 2 * rows, HD), BF),
            pltpu.VMEM((4, 1, 2 * HD), F32),
            pltpu.VMEM((4, 1, 2 * HD), F32),
            pltpu.VMEM((4, HD, 2 * HD), F32),
            pltpu.VMEM((2, HD + 16, 2 * HD), BF),
            pltpu.VMEM((2, HD + 16, 2 * HD), BF),
            pltpu.VMEM((2, rows, G * HD), BF),
            pltpu.VMEM((nzh, 2, w.shape[0], width), BF),
            pltpu.VMEM((rows, width), BF),
            pltpu.VMEM((2, half, width), F32),
            piece, piece, piece, piece, piece, piece, piece, piece,
            pltpu.VMEM((rows, width), BF),
            dma((3,)), dma((ny, 2, 2)), dma((ny, 2, 2)),
            dma(()), dma(()), dma((2,)), dma((2,)),
            dma((nzh,)), dma((nzh,)), dma((nzh,)),
            dma(()), dma(()),
            dma((2, PARTS)), dma((2, PARTS)), dma((2, PARTS)), dma((2, PARTS)), dma((2, PARTS)), dma((2, PARTS)),
            dma((2, PARTS)), dma((2, PARTS)), dma(()), dma(()), dma((2, PARTS)),
        ],
        compiler_params=pltpu.CompilerParams(
            collective_id=0, has_side_effects=True, vmem_limit_bytes=64 * 1024 * 1024 - 70000
        ),
    )(row_offsets, q, k, v, res, w)
    return out[None]


def solution(mesh):
    placed = (
        P("section"),
        P("section", "ctx", "tp"),
        P("section", "ctx", "tp"),
        P("section", "ctx", "tp"),
        P("section", "ctx", "tp"),
        P("section", "tp", None),
    )
    ny, nzh, nx = mesh.shape["ctx"] // 2, mesh.shape["tp"] // 2, mesh.shape["section"]
    return jax.shard_map(
        functools.partial(on_device, ny, nzh, nx),
        mesh=mesh, in_specs=placed, out_specs=P("section", "ctx", "tp"), check_vma=False,
    )
```

```python
import functools

import jax
import jax.numpy as jnp
from jax import lax
from jax.experimental import pallas as pl
from jax.experimental.pallas import tpu as pltpu
from jax.sharding import PartitionSpec as P

HD = 128
G = 4
NEG = -(2.0**100)
LOG2E = 1.4426950408889634
PARTS = 2
MESH = pl.DeviceIdType.MESH
BF = jnp.bfloat16
F32 = jnp.float32


def kernel(
    ny, nzh, nx,
    off_ref, q_ref, k_ref, v_ref, res_ref, w_ref, o_ref,
    kvb, vt, qin, qs, m_ref, l_ref, acc, snd, rcv, att, wbuf, resv, keep,
    far_s, far_r, near_s, near_r, mix_s, mix_r, own_s, own_r, fin,
    loc, kv_s, kv_r, q_s, q_r, a_s, a_r, w_l, w_s, w_r, t_s, t_r,
    far_ss, far_rs, near_ss, near_rs, mix_ss, mix_rs, own_ss, own_rs, r_s, r_r, o_l,
):
    rows = q_ref.shape[0]
    klen = k_ref.shape[0]
    width = res_ref.shape[1]
    half = rows // 2
    part = half // PARTS
    two = 2 * HD
    hops = ny // 2
    cut = (klen // HD + 1) // 2 * HD
    spans = ((0, cut), (cut, klen - cut))

    ctx = lax.axis_index("ctx")
    tp = lax.axis_index("tp")
    x = lax.axis_index("section")
    y, zl = ctx // 2, ctx % 2
    zh, co = tp // 2, tp % 2
    y_next = {"ctx": ((y + 1) % ny) * 2 + zl}
    y_prev = {"ctx": ((y + ny - 1) % ny) * 2 + zl}
    ring = (y_next, y_prev)
    z_mate = {"ctx": y * 2 + 1 - zl}
    core_mate = {"tp": zh * 2 + 1 - co}
    zh_next = {"tp": ((zh + 1) % nzh) * 2 + co}
    zh_prev = {"tp": ((zh + nzh - 1) % nzh) * 2 + co}
    zring = (zh_next, zh_prev)
    x_next = {"section": (x + 1) % nx}
    x_prev = {"section": (x + nx - 1) % nx}
    landing = tuple({**x_next, **z} for z in zring)
    leaving = tuple({**x_prev, **z} for z in zring)

    def remote(src, dst, s, r, where):
        return pltpu.make_async_remote_copy(
            src_ref=src, dst_ref=dst, send_sem=s, recv_sem=r, device_id=where, device_id_type=MESH
        )

    def wcols(block, core):
        return pl.ds(pl.multiple_of(block * 2 * width + core * width, width), width)

    local_k = pltpu.make_async_copy(k_ref, kvb.at[0, 0], loc.at[0])
    local_v = pltpu.make_async_copy(v_ref, kvb.at[0, 1], loc.at[1])
    local_q = pltpu.make_async_copy(q_ref, qin.at[0], loc.at[2])
    local_w = [
        pltpu.make_async_copy(w_ref.at[:, wcols(b, co)], wbuf.at[b, co], w_l.at[b]) for b in range(nzh)
    ]
    local_q.start()
    local_k.start()
    local_v.start()

    barrier = pltpu.get_barrier_semaphore()
    greet = (y_next, y_prev, z_mate, core_mate, zh_next, zh_prev, x_next, x_prev) + landing + leaving
    for where in greet:
        pl.semaphore_signal(barrier, inc=1, device_id=where, device_id_type=MESH)
    pl.semaphore_wait(barrier, len(greet))

    def hop(src, slot, i, way, kind):
        at = pl.ds(*spans[i])
        dst = kvb.at[slot, kind, at]
        return remote(src.at[at], dst, kv_s.at[slot, i, kind], kv_r.at[slot, i, kind], ring[way])

    send_q = remote(q_ref, qin.at[1], q_s, q_r, z_mate)
    for i in (0, 1):
        for kind in (0, 1):
            for way in (0, 1):
                hop((k_ref, v_ref)[kind], 1 + way, i, way, kind).start()
        if i == 0:
            send_q.start()
    send_w = [
        remote(w_ref.at[:, wcols(b, 1 - co)], wbuf.at[b, co], w_s.at[b], w_r.at[b], core_mate)
        for b in range(nzh)
    ]
    for c in send_w:
        c.start()
    for c in local_w:
        c.start()
    send_r = remote(res_ref, resv, r_s, r_r, x_next)
    send_r.start()

    m_ref[...] = jnp.full(m_ref.shape, NEG, F32)
    l_ref[...] = jnp.zeros(l_ref.shape, F32)
    acc[...] = jnp.zeros(acc.shape, F32)
    lane_row = lax.broadcasted_iota(jnp.int32, (1, two), 1) % rows
    offset = off_ref[0]
    stat_row = lax.broadcasted_iota(jnp.int32, (16, two), 0)
    scale = HD ** (-0.5) * LOG2E

    def lay_queries(c):
        for g in (0, 1):
            for h in (0, 1):
                col = (2 * g + h) * HD
                qs[2 * c + g, h * rows : (h + 1) * rows, :] = qin[c, :, col : col + HD]

    def turn(slot, start, size):
        vt[slot, :, start : start + size] = kvb[slot, 1, start : start + size, :].T

    def attend(slot, block, start, size, first, last):
        key_pos = (block * 2 + zl) * klen + start + lax.broadcasted_iota(jnp.int32, (size, two), 0)

        def row_class(other, carry):
            row_pos = offset + (y * 2 + zl + other * (1 - 2 * zl)) * rows + lane_row
            visible = key_pos <= row_pos
            for g in (2 * other, 2 * other + 1):
                scores = lax.dot_general(
                    kvb[slot, 0, start : start + size, :], qs[g], (((1,), (1,)), ((), ())), preferred_element_type=F32
                )
                scores = jnp.where(visible, scores, NEG)
                top_old = m_ref[g]
                top = jnp.maximum(jnp.max(scores, axis=0, keepdims=True).astype(BF).astype(F32), top_old)
                weights = jnp.exp2((scores - top) * scale)
                fade = jnp.exp2((top_old - top) * scale)
                m_ref[g] = top
                l_ref[g] = l_ref[g] * fade + jnp.sum(weights, axis=0, keepdims=True)
                mixed = jnp.dot(
                    vt[slot, :, start : start + size], weights.astype(BF), preferred_element_type=F32
                )
                acc[g] = acc[g] * fade + mixed
            return carry

        lax.fori_loop(first, last, row_class, 0)

    def arrive(slot, i, way, kind):
        return hop(kvb.at[slot, kind], slot, i, way, kind)

    local_q.wait()
    lay_queries(0)
    local_k.wait()
    local_v.wait()
    turn(0, 0, klen)

    def forward(h, i, kind):
        for way in (0, 1):
            slot = 2 * h - 1 + way
            arrive(slot, i, way, kind).wait_recv()
            dest = 2 * h + 1 if way == 0 else jnp.minimum(2 * h + 2, ny - 1)
            onward = hop(kvb.at[slot, kind], dest, i, way, kind)
            if way == i:
                onward.start()
            else:

                @pl.when(h < hops - 1)
                def _():
                    onward.start()

    def round_trip(h, carry):
        forward(h, 0, 0)

        @pl.when(h > 1)
        def _():
            attend(2 * h - 3, (y + ny + 1 - h) % ny, 0, klen, 1, 2)

        forward(h, 0, 1)

        @pl.when(h > 1)
        def _():
            turn(2 * h - 2, 0, klen)

        attend(2 * h - 2, (y + h - 1) % ny, 0, klen, 0, 1)
        forward(h, 1, 0)

        @pl.when(h == 1)
        def _():
            send_q.wait_recv()
            lay_queries(1)

        attend(2 * h - 2, (y + h - 1) % ny, 0, klen, 1, 2)
        forward(h, 1, 1)
        turn(2 * h - 1, 0, klen)
        attend(2 * h - 1, (y + ny - h) % ny, 0, klen, 0, 1)
        return carry

    lax.fori_loop(1, hops, round_trip, 0)

    last = ny - 1
    far_block = (y + hops) % ny
    attend(last - 2, (y + ny + 1 - hops) % ny, 0, klen, 1, 2)
    turn(last - 1, 0, klen)
    attend(last - 1, (y + hops - 1) % ny, 0, klen, 0, 2)
    for kind in (0, 1):
        arrive(last, 0, 0, kind).wait_recv()
    turn(last, 0, cut)
    attend(last, far_block, 0, cut, 0, 2)
    for kind in (0, 1):
        arrive(last, 1, 1, kind).wait_recv()
    turn(last, cut, klen - cut)
    attend(last, far_block, cut, klen - cut, 1, 2)
    send_a = [remote(snd.at[g], rcv.at[g], a_s.at[g], a_r.at[g], z_mate) for g in (0, 1)]
    for g in (0, 1):
        snd[g, 0:HD, :] = acc[2 + g].astype(BF)
        total = l_ref[2 + g]
        high = total.astype(BF).astype(F32)
        packed = jnp.where(
            stat_row == 0,
            m_ref[2 + g],
            jnp.where(stat_row == 1, high, jnp.where(stat_row == 2, total - high, 0.0)),
        )
        snd[g, HD:, :] = packed.astype(BF)
        send_a[g].start()
    attend(last, far_block, cut, klen - cut, 0, 1)
    for g in (0, 1):
        send_a[g].wait_recv()
        stats = rcv[g, HD:, :].astype(F32)
        top_in = stats[0:1]
        sum_in = stats[1:2] + stats[2:3]
        top_new = jnp.maximum(top_in, m_ref[g])
        f_in = jnp.exp2((top_in - top_new) * scale)
        f_own = jnp.exp2((m_ref[g] - top_new) * scale)
        sum_new = sum_in * f_in + l_ref[g] * f_own
        head = (rcv[g, 0:HD, :].astype(F32) * f_in + acc[g] * f_own) / sum_new
        for h in (0, 1):
            col = (2 * g + h) * HD
            att[co, :, col : col + HD] = head[:, h * rows : (h + 1) * rows].T.astype(BF)

    send_t = remote(att.at[co], att.at[co], t_s, t_r, core_mate)
    send_t.start()
    for c in local_w:
        c.wait()
    for c in send_w:
        c.wait_recv()

    def share(core, away):
        return jnp.dot(att[core], wbuf[(zh + away) % nzh, core], preferred_element_type=F32)

    first_half = share(co, 2)
    send_t.wait_recv()

    def product(away):
        return share(0, away) + share(1, away)

    def span(i, j):
        return slice(i * half + j * part, i * half + (j + 1) * part)

    far_cp = [[remote(far_s.at[i, j], far_r.at[i, j], far_ss.at[i, j], far_rs.at[i, j], zring[i]) for j in range(PARTS)] for i in (0, 1)]
    near_cp = [[remote(near_s.at[i, j], near_r.at[i, j], near_ss.at[i, j], near_rs.at[i, j], landing[i]) for j in range(PARTS)] for i in (0, 1)]
    mix_cp = [[remote(mix_s.at[i, j], mix_r.at[i, j], mix_ss.at[i, j], mix_rs.at[i, j], landing[i]) for j in range(PARTS)] for i in (0, 1)]
    own_cp = [[remote(own_s.at[i, j], own_r.at[i, j], own_ss.at[i, j], own_rs.at[i, j], x_next) for j in range(PARTS)] for i in (0, 1)]
    out_cp = [[pltpu.make_async_copy(fin.at[span(i, j)], o_ref.at[span(i, j)], o_l.at[i, j]) for j in range(PARTS)] for i in (0, 1)]

    opposite = first_half + share(1 - co, 2)
    for j in range(PARTS):
        for i in (0, 1):
            far_s[i, j] = opposite[span(i, j)].astype(BF)
            far_cp[i][j].start()
    own = product(0)
    for j in range(PARTS):
        for i in (0, 1):
            own_s[i, j] = own[span(i, j)].astype(BF)
            own_cp[i][j].start()
    for i in (0, 1):
        out = product(1 if i == 0 else nzh - 1)
        keep[i] = out[i * half : (i + 1) * half]
        for j in range(PARTS):
            near_s[i, j] = out[span(1 - i, j)].astype(BF)
            near_cp[i][j].start()
    for j in range(PARTS):
        for i in (0, 1):
            far_cp[i][j].wait_recv()
            mix_s[i, j] = (keep[i, j * part : (j + 1) * part] + far_r[i, j].astype(F32)).astype(BF)
            mix_cp[i][j].start()
    send_r.wait_recv()
    for j in range(PARTS):
        for i in (0, 1):
            own_cp[i][j].wait_recv()
            near_cp[1 - i][j].wait_recv()
            mix_cp[i][j].wait_recv()
            summed = own_r[i, j].astype(F32) + near_r[1 - i, j].astype(F32) + mix_r[i, j].astype(F32)
            fin[span(i, j)] = (resv[span(i, j)].astype(F32) + summed).astype(BF)
            out_cp[i][j].start()

    send_q.wait_send()
    send_r.wait_send()
    for c in send_w:
        c.wait_send()
    send_t.wait_send()
    for c in send_a:
        c.wait_send()

    def drain(slot, carry):
        for i in (0, 1):
            for kind in (0, 1):
                arrive(slot, i, 0, kind).wait_send()
        return carry

    lax.fori_loop(1, ny, drain, 0)
    for i in (0, 1):
        for j in range(PARTS):
            far_cp[i][j].wait_send()
            own_cp[i][j].wait_send()
            near_cp[i][j].wait_send()
            mix_cp[i][j].wait_send()
            out_cp[i][j].wait()


def on_device(ny, nzh, nx, row_offsets, queries, cache_keys, cache_values, residual, out_weight):
    q, k, v, res, w = queries[0], cache_keys[0], cache_values[0], residual[0], out_weight[0]
    rows, klen, width = q.shape[0], k.shape[0], res.shape[1]
    half = rows // 2
    part = half // PARTS
    dma = pltpu.SemaphoreType.DMA
    piece = pltpu.VMEM((2, PARTS, part, width), BF)
    any_spec = pl.BlockSpec(memory_space=pl.ANY)
    out = pl.pallas_call(
        functools.partial(kernel, ny, nzh, nx),
        out_shape=jax.ShapeDtypeStruct(res.shape, BF),
        in_specs=[pl.BlockSpec(memory_space=pltpu.SMEM)] + [any_spec] * 5,
        out_specs=any_spec,
        scratch_shapes=[
            pltpu.VMEM((ny, 2, klen, HD), BF),
            pltpu.VMEM((ny, HD, klen), BF),
            pltpu.VMEM((2, rows, G * HD), BF),
            pltpu.VMEM((4, 2 * rows, HD), BF),
            pltpu.VMEM((4, 1, 2 * HD), F32),
            pltpu.VMEM((4, 1, 2 * HD), F32),
            pltpu.VMEM((4, HD, 2 * HD), F32),
            pltpu.VMEM((2, HD + 16, 2 * HD), BF),
            pltpu.VMEM((2, HD + 16, 2 * HD), BF),
            pltpu.VMEM((2, rows, G * HD), BF),
            pltpu.VMEM((nzh, 2, w.shape[0], width), BF),
            pltpu.VMEM((rows, width), BF),
            pltpu.VMEM((2, half, width), F32),
            piece, piece, piece, piece, piece, piece, piece, piece,
            pltpu.VMEM((rows, width), BF),
            dma((3,)), dma((ny, 2, 2)), dma((ny, 2, 2)),
            dma(()), dma(()), dma((2,)), dma((2,)),
            dma((nzh,)), dma((nzh,)), dma((nzh,)),
            dma(()), dma(()),
            dma((2, PARTS)), dma((2, PARTS)), dma((2, PARTS)), dma((2, PARTS)), dma((2, PARTS)), dma((2, PARTS)),
            dma((2, PARTS)), dma((2, PARTS)), dma(()), dma(()), dma((2, PARTS)),
        ],
        compiler_params=pltpu.CompilerParams(
            collective_id=0, has_side_effects=True, vmem_limit_bytes=64 * 1024 * 1024 - 70000
        ),
    )(row_offsets, q, k, v, res, w)
    return out[None]


def solution(mesh):
    placed = (
        P("section"),
        P("section", "ctx", "tp"),
        P("section", "ctx", "tp"),
        P("section", "ctx", "tp"),
        P("section", "ctx", "tp"),
        P("section", "tp", None),
    )
    ny, nzh, nx = mesh.shape["ctx"] // 2, mesh.shape["tp"] // 2, mesh.shape["section"]
    return jax.shard_map(
        functools.partial(on_device, ny, nzh, nx),
        mesh=mesh, in_specs=placed, out_specs=P("section", "ctx", "tp"), check_vma=False,
    )
```

```python
import functools

import jax
import jax.numpy as jnp
from jax import lax
from jax.experimental import pallas as pl
from jax.experimental.pallas import tpu as pltpu
from jax.sharding import PartitionSpec as P

HD = 128
G = 4
NEG = -(2.0**100)
LOG2E = 1.4426950408889634
PARTS = 2
MESH = pl.DeviceIdType.MESH
BF = jnp.bfloat16
F32 = jnp.float32


def kernel(
    ny, nzh, nx,
    off_ref, q_ref, k_ref, v_ref, res_ref, w_ref, o_ref,
    kvb, vt, qin, qs, m_ref, l_ref, acc, snd, rcv, att, wbuf, resv, keep,
    far_s, far_r, near_s, near_r, mix_s, mix_r, own_s, own_r, fin,
    loc, kv_s, kv_r, q_s, q_r, a_s, a_r, w_l, w_s, w_r, t_s, t_r,
    far_ss, far_rs, near_ss, near_rs, mix_ss, mix_rs, own_ss, own_rs, r_s, r_r, o_l,
):
    rows = q_ref.shape[0]
    klen = k_ref.shape[0]
    width = res_ref.shape[1]
    half = rows // 2
    part = half // PARTS
    two = 2 * HD
    hops = ny // 2
    cut = (klen // HD + 1) // 2 * HD
    spans = ((0, cut), (cut, klen - cut))

    ctx = lax.axis_index("ctx")
    tp = lax.axis_index("tp")
    x = lax.axis_index("section")
    y, zl = ctx // 2, ctx % 2
    zh, co = tp // 2, tp % 2
    y_next = {"ctx": ((y + 1) % ny) * 2 + zl}
    y_prev = {"ctx": ((y + ny - 1) % ny) * 2 + zl}
    ring = (y_next, y_prev)
    z_mate = {"ctx": y * 2 + 1 - zl}
    cross_to = {"ctx": ((y + ny - 1) % ny) * 2 + 1 - zl}
    cross_from = {"ctx": ((y + 1) % ny) * 2 + 1 - zl}
    core_mate = {"tp": zh * 2 + 1 - co}
    zh_next = {"tp": ((zh + 1) % nzh) * 2 + co}
    zh_prev = {"tp": ((zh + nzh - 1) % nzh) * 2 + co}
    zring = (zh_next, zh_prev)
    x_next = {"section": (x + 1) % nx}
    x_prev = {"section": (x + nx - 1) % nx}
    landing = tuple({**x_next, **z} for z in zring)
    leaving = tuple({**x_prev, **z} for z in zring)

    def remote(src, dst, s, r, where):
        return pltpu.make_async_remote_copy(
            src_ref=src, dst_ref=dst, send_sem=s, recv_sem=r, device_id=where, device_id_type=MESH
        )

    def wcols(block, core):
        return pl.ds(pl.multiple_of(block * 2 * width + core * width, width), width)

    local_k = pltpu.make_async_copy(k_ref, kvb.at[0, 0], loc.at[0])
    local_v = pltpu.make_async_copy(v_ref, kvb.at[0, 1], loc.at[1])
    local_q = pltpu.make_async_copy(q_ref, qin.at[0], loc.at[2])
    local_w = [
        pltpu.make_async_copy(w_ref.at[:, wcols(b, co)], wbuf.at[b, co], w_l.at[b]) for b in range(nzh)
    ]
    local_q.start()
    local_k.start()
    local_v.start()

    barrier = pltpu.get_barrier_semaphore()
    greet = (y_next, y_prev, z_mate, cross_to, cross_from, core_mate, zh_next, zh_prev, x_next, x_prev) + landing + leaving
    for where in greet:
        pl.semaphore_signal(barrier, inc=1, device_id=where, device_id_type=MESH)
    pl.semaphore_wait(barrier, len(greet))

    def hop(src, slot, i, way, kind):
        at = pl.ds(*spans[i])
        dst = kvb.at[slot, kind, at]
        return remote(src.at[at], dst, kv_s.at[slot, i, kind], kv_r.at[slot, i, kind], ring[way])

    send_q = remote(q_ref, qin.at[1], q_s, q_r, z_mate)
    for i in (0, 1):
        for kind in (0, 1):
            for way in (0, 1):
                hop((k_ref, v_ref)[kind], 1 + way, i, way, kind).start()
        if i == 0:
            send_q.start()
    send_w = [
        remote(w_ref.at[:, wcols(b, 1 - co)], wbuf.at[b, co], w_s.at[b], w_r.at[b], core_mate)
        for b in range(nzh)
    ]
    for c in send_w:
        c.start()
    for c in local_w:
        c.start()
    send_r = remote(res_ref, resv, r_s, r_r, x_next)
    send_r.start()

    m_ref[...] = jnp.full(m_ref.shape, NEG, F32)
    l_ref[...] = jnp.zeros(l_ref.shape, F32)
    acc[...] = jnp.zeros(acc.shape, F32)
    lane_row = lax.broadcasted_iota(jnp.int32, (1, two), 1) % rows
    offset = off_ref[0]
    stat_row = lax.broadcasted_iota(jnp.int32, (16, two), 0)
    scale = HD ** (-0.5) * LOG2E

    def lay_queries(c):
        for g in (0, 1):
            for h in (0, 1):
                col = (2 * g + h) * HD
                qs[2 * c + g, h * rows : (h + 1) * rows, :] = qin[c, :, col : col + HD]

    def cross_hop(kind):
        at = pl.ds(*spans[1])
        return remote(
            kvb.at[ny - 2, kind, at], kvb.at[ny, kind, at], kv_s.at[ny, 1, kind], kv_r.at[ny, 1, kind], cross_to
        )

    def turn(slot, start, size):
        vt[slot, :, start : start + size] = kvb[slot, 1, start : start + size, :].T

    def attend(slot, block, start, size, first, last, side=0):
        key_pos = (block * 2 + zl + side * (1 - 2 * zl)) * klen + start + lax.broadcasted_iota(jnp.int32, (size, two), 0)

        def row_class(other, carry):
            row_pos = offset + (y * 2 + zl + other * (1 - 2 * zl)) * rows + lane_row
            visible = key_pos <= row_pos
            for g in (2 * other, 2 * other + 1):
                scores = lax.dot_general(
                    kvb[slot, 0, start : start + size, :], qs[g], (((1,), (1,)), ((), ())), preferred_element_type=F32
                )
                scores = jnp.where(visible, scores, NEG)
                top_old = m_ref[g]
                top = jnp.maximum(jnp.max(scores, axis=0, keepdims=True).astype(BF).astype(F32), top_old)
                weights = jnp.exp2((scores - top) * scale)
                fade = jnp.exp2((top_old - top) * scale)
                m_ref[g] = top
                l_ref[g] = l_ref[g] * fade + jnp.sum(weights, axis=0, keepdims=True)
                mixed = jnp.dot(
                    vt[slot, :, start : start + size], weights.astype(BF), preferred_element_type=F32
                )
                acc[g] = acc[g] * fade + mixed
            return carry

        lax.fori_loop(first, last, row_class, 0)

    def arrive(slot, i, way, kind):
        return hop(kvb.at[slot, kind], slot, i, way, kind)

    local_q.wait()
    lay_queries(0)
    local_k.wait()
    local_v.wait()
    turn(0, 0, klen)

    def forward(h, i, kind):
        for way in (0, 1):
            slot = 2 * h - 1 + way
            arrive(slot, i, way, kind).wait_recv()
            dest = 2 * h + 1 if way == 0 else jnp.minimum(2 * h + 2, ny - 1)
            onward = hop(kvb.at[slot, kind], dest, i, way, kind)
            if way == i:
                onward.start()
                if way == 1:

                    @pl.when(h == hops - 1)
                    def _():
                        cross_hop(kind).start()

            else:

                @pl.when(h < hops - 1)
                def _():
                    onward.start()

    def round_trip(h, carry):
        forward(h, 0, 0)

        @pl.when(h > 1)
        def _():
            attend(2 * h - 3, (y + ny + 1 - h) % ny, 0, klen, 1, 2)

        forward(h, 0, 1)

        @pl.when(h > 1)
        def _():
            turn(2 * h - 2, 0, klen)

        attend(2 * h - 2, (y + h - 1) % ny, 0, klen, 0, 1)
        forward(h, 1, 0)

        @pl.when(h == 1)
        def _():
            send_q.wait_recv()
            lay_queries(1)

        attend(2 * h - 2, (y + h - 1) % ny, 0, klen, 1, 2)
        forward(h, 1, 1)
        turn(2 * h - 1, 0, klen)
        attend(2 * h - 1, (y + ny - h) % ny, 0, klen, 0, 1)
        return carry

    lax.fori_loop(1, hops, round_trip, 0)

    last = ny - 1
    far_block = (y + hops) % ny
    attend(last - 2, (y + ny + 1 - hops) % ny, 0, klen, 1, 2)
    turn(last - 1, 0, klen)
    attend(last - 1, (y + hops - 1) % ny, 0, klen, 0, 2)
    for kind in (0, 1):
        arrive(last, 0, 0, kind).wait_recv()
    turn(last, 0, cut)
    attend(last, far_block, 0, cut, 0, 2)
    send_a = [remote(snd.at[g], rcv.at[g], a_s.at[g], a_r.at[g], z_mate) for g in (0, 1)]
    for g in (0, 1):
        snd[g, 0:HD, :] = acc[2 + g].astype(BF)
        total = l_ref[2 + g]
        high = total.astype(BF).astype(F32)
        packed = jnp.where(
            stat_row == 0,
            m_ref[2 + g],
            jnp.where(stat_row == 1, high, jnp.where(stat_row == 2, total - high, 0.0)),
        )
        snd[g, HD:, :] = packed.astype(BF)
        send_a[g].start()
    for kind in (0, 1):
        arrive(last, 1, 1, kind).wait_recv()
    turn(last, cut, klen - cut)
    attend(last, far_block, cut, klen - cut, 0, 1)
    for kind in (0, 1):
        cross_hop(kind).wait_recv()
    turn(ny, cut, klen - cut)
    attend(ny, far_block, cut, klen - cut, 0, 1, 1)
    for g in (0, 1):
        send_a[g].wait_recv()
        stats = rcv[g, HD:, :].astype(F32)
        top_in = stats[0:1]
        sum_in = stats[1:2] + stats[2:3]
        top_new = jnp.maximum(top_in, m_ref[g])
        f_in = jnp.exp2((top_in - top_new) * scale)
        f_own = jnp.exp2((m_ref[g] - top_new) * scale)
        sum_new = sum_in * f_in + l_ref[g] * f_own
        head = (rcv[g, 0:HD, :].astype(F32) * f_in + acc[g] * f_own) / sum_new
        for h in (0, 1):
            col = (2 * g + h) * HD
            att[co, :, col : col + HD] = head[:, h * rows : (h + 1) * rows].T.astype(BF)

    send_t = remote(att.at[co], att.at[co], t_s, t_r, core_mate)
    send_t.start()
    for c in local_w:
        c.wait()
    for c in send_w:
        c.wait_recv()

    def share(core, away):
        return jnp.dot(att[core], wbuf[(zh + away) % nzh, core], preferred_element_type=F32)

    first_half = share(co, 2)
    send_t.wait_recv()

    def product(away):
        return share(0, away) + share(1, away)

    def span(i, j):
        return slice(i * half + j * part, i * half + (j + 1) * part)

    far_cp = [[remote(far_s.at[i, j], far_r.at[i, j], far_ss.at[i, j], far_rs.at[i, j], zring[i]) for j in range(PARTS)] for i in (0, 1)]
    near_cp = [[remote(near_s.at[i, j], near_r.at[i, j], near_ss.at[i, j], near_rs.at[i, j], landing[i]) for j in range(PARTS)] for i in (0, 1)]
    mix_cp = [[remote(mix_s.at[i, j], mix_r.at[i, j], mix_ss.at[i, j], mix_rs.at[i, j], landing[i]) for j in range(PARTS)] for i in (0, 1)]
    own_cp = [[remote(own_s.at[i, j], own_r.at[i, j], own_ss.at[i, j], own_rs.at[i, j], x_next) for j in range(PARTS)] for i in (0, 1)]
    out_cp = [[pltpu.make_async_copy(fin.at[span(i, j)], o_ref.at[span(i, j)], o_l.at[i, j]) for j in range(PARTS)] for i in (0, 1)]

    opposite = first_half + share(1 - co, 2)
    for j in range(PARTS):
        for i in (0, 1):
            far_s[i, j] = opposite[span(i, j)].astype(BF)
            far_cp[i][j].start()
    own = product(0)
    for j in range(PARTS):
        for i in (0, 1):
            own_s[i, j] = own[span(i, j)].astype(BF)
            own_cp[i][j].start()
    for i in (0, 1):
        out = product(1 if i == 0 else nzh - 1)
        keep[i] = out[i * half : (i + 1) * half]
        for j in range(PARTS):
            near_s[i, j] = out[span(1 - i, j)].astype(BF)
            near_cp[i][j].start()
    for j in range(PARTS):
        for i in (0, 1):
            far_cp[i][j].wait_recv()
            mix_s[i, j] = (keep[i, j * part : (j + 1) * part] + far_r[i, j].astype(F32)).astype(BF)
            mix_cp[i][j].start()
    send_r.wait_recv()
    for j in range(PARTS):
        for i in (0, 1):
            own_cp[i][j].wait_recv()
            near_cp[1 - i][j].wait_recv()
            mix_cp[i][j].wait_recv()
            summed = own_r[i, j].astype(F32) + near_r[1 - i, j].astype(F32) + mix_r[i, j].astype(F32)
            fin[span(i, j)] = (resv[span(i, j)].astype(F32) + summed).astype(BF)
            out_cp[i][j].start()

    send_q.wait_send()
    send_r.wait_send()
    for c in send_w:
        c.wait_send()
    send_t.wait_send()
    for c in send_a:
        c.wait_send()

    def drain(slot, carry):
        for i in (0, 1):
            for kind in (0, 1):
                arrive(slot, i, 0, kind).wait_send()
        return carry

    lax.fori_loop(1, ny, drain, 0)
    for kind in (0, 1):
        cross_hop(kind).wait_send()
    for i in (0, 1):
        for j in range(PARTS):
            far_cp[i][j].wait_send()
            own_cp[i][j].wait_send()
            near_cp[i][j].wait_send()
            mix_cp[i][j].wait_send()
            out_cp[i][j].wait()


def on_device(ny, nzh, nx, row_offsets, queries, cache_keys, cache_values, residual, out_weight):
    q, k, v, res, w = queries[0], cache_keys[0], cache_values[0], residual[0], out_weight[0]
    rows, klen, width = q.shape[0], k.shape[0], res.shape[1]
    half = rows // 2
    part = half // PARTS
    dma = pltpu.SemaphoreType.DMA
    piece = pltpu.VMEM((2, PARTS, part, width), BF)
    any_spec = pl.BlockSpec(memory_space=pl.ANY)
    out = pl.pallas_call(
        functools.partial(kernel, ny, nzh, nx),
        out_shape=jax.ShapeDtypeStruct(res.shape, BF),
        in_specs=[pl.BlockSpec(memory_space=pltpu.SMEM)] + [any_spec] * 5,
        out_specs=any_spec,
        scratch_shapes=[
            pltpu.VMEM((ny + 1, 2, klen, HD), BF),
            pltpu.VMEM((ny + 1, HD, klen), BF),
            pltpu.VMEM((2, rows, G * HD), BF),
            pltpu.VMEM((4, 2 * rows, HD), BF),
            pltpu.VMEM((4, 1, 2 * HD), F32),
            pltpu.VMEM((4, 1, 2 * HD), F32),
            pltpu.VMEM((4, HD, 2 * HD), F32),
            pltpu.VMEM((2, HD + 16, 2 * HD), BF),
            pltpu.VMEM((2, HD + 16, 2 * HD), BF),
            pltpu.VMEM((2, rows, G * HD), BF),
            pltpu.VMEM((nzh, 2, w.shape[0], width), BF),
            pltpu.VMEM((rows, width), BF),
            pltpu.VMEM((2, half, width), F32),
            piece, piece, piece, piece, piece, piece, piece, piece,
            pltpu.VMEM((rows, width), BF),
            dma((3,)), dma((ny + 1, 2, 2)), dma((ny + 1, 2, 2)),
            dma(()), dma(()), dma((2,)), dma((2,)),
            dma((nzh,)), dma((nzh,)), dma((nzh,)),
            dma(()), dma(()),
            dma((2, PARTS)), dma((2, PARTS)), dma((2, PARTS)), dma((2, PARTS)), dma((2, PARTS)), dma((2, PARTS)),
            dma((2, PARTS)), dma((2, PARTS)), dma(()), dma(()), dma((2, PARTS)),
        ],
        compiler_params=pltpu.CompilerParams(
            collective_id=0, has_side_effects=True, vmem_limit_bytes=64 * 1024 * 1024 - 70000
        ),
    )(row_offsets, q, k, v, res, w)
    return out[None]


def solution(mesh):
    placed = (
        P("section"),
        P("section", "ctx", "tp"),
        P("section", "ctx", "tp"),
        P("section", "ctx", "tp"),
        P("section", "ctx", "tp"),
        P("section", "tp", None),
    )
    ny, nzh, nx = mesh.shape["ctx"] // 2, mesh.shape["tp"] // 2, mesh.shape["section"]
    return jax.shard_map(
        functools.partial(on_device, ny, nzh, nx),
        mesh=mesh, in_specs=placed, out_specs=P("section", "ctx", "tp"), check_vma=False,
    )
```

```python
import functools

import jax
import jax.numpy as jnp
from jax import lax
from jax.experimental import pallas as pl
from jax.experimental.pallas import tpu as pltpu
from jax.sharding import PartitionSpec as P

HD = 128
G = 4
NEG = -(2.0**100)
LOG2E = 1.4426950408889634
PARTS = 4
MESH = pl.DeviceIdType.MESH
BF = jnp.bfloat16
F32 = jnp.float32


def kernel(
    ny, nzh, nx,
    off_ref, q_ref, k_ref, v_ref, res_ref, w_ref, o_ref,
    kvb, vt, qin, qs, m_ref, l_ref, acc, snd, rcv, att, wbuf, resv, keep,
    far_s, far_r, near_s, near_r, mix_s, mix_r, own_s, own_r, fin,
    loc, kv_s, kv_r, q_s, q_r, a_s, a_r, w_l, w_s, w_r, t_s, t_r,
    far_ss, far_rs, near_ss, near_rs, mix_ss, mix_rs, own_ss, own_rs, r_s, r_r, o_l,
):
    rows = q_ref.shape[0]
    klen = k_ref.shape[0]
    width = res_ref.shape[1]
    half = rows // 2
    part = half // PARTS
    two = 2 * HD
    hops = ny // 2
    cut = (klen // HD + 1) // 2 * HD
    spans = ((0, cut), (cut, klen - cut))

    ctx = lax.axis_index("ctx")
    tp = lax.axis_index("tp")
    x = lax.axis_index("section")
    y, zl = ctx // 2, ctx % 2
    zh, co = tp // 2, tp % 2
    y_next = {"ctx": ((y + 1) % ny) * 2 + zl}
    y_prev = {"ctx": ((y + ny - 1) % ny) * 2 + zl}
    ring = (y_next, y_prev)
    z_mate = {"ctx": y * 2 + 1 - zl}
    cross_to = {"ctx": ((y + ny - 1) % ny) * 2 + 1 - zl}
    cross_from = {"ctx": ((y + 1) % ny) * 2 + 1 - zl}
    core_mate = {"tp": zh * 2 + 1 - co}
    zh_next = {"tp": ((zh + 1) % nzh) * 2 + co}
    zh_prev = {"tp": ((zh + nzh - 1) % nzh) * 2 + co}
    zring = (zh_next, zh_prev)
    x_next = {"section": (x + 1) % nx}
    x_prev = {"section": (x + nx - 1) % nx}
    landing = tuple({**x_next, **z} for z in zring)
    leaving = tuple({**x_prev, **z} for z in zring)

    def remote(src, dst, s, r, where):
        return pltpu.make_async_remote_copy(
            src_ref=src, dst_ref=dst, send_sem=s, recv_sem=r, device_id=where, device_id_type=MESH
        )

    def wcols(block, core):
        return pl.ds(pl.multiple_of(block * 2 * width + core * width, width), width)

    local_k = pltpu.make_async_copy(k_ref, kvb.at[0, 0], loc.at[0])
    local_v = pltpu.make_async_copy(v_ref, kvb.at[0, 1], loc.at[1])
    local_q = pltpu.make_async_copy(q_ref, qin.at[0], loc.at[2])
    local_w = [
        pltpu.make_async_copy(w_ref.at[:, wcols(b, co)], wbuf.at[b, co], w_l.at[b]) for b in range(nzh)
    ]
    local_q.start()
    local_k.start()
    local_v.start()

    barrier = pltpu.get_barrier_semaphore()
    greet = (y_next, y_prev, z_mate, cross_to, cross_from, core_mate, zh_next, zh_prev, x_next, x_prev) + landing + leaving
    for where in greet:
        pl.semaphore_signal(barrier, inc=1, device_id=where, device_id_type=MESH)
    pl.semaphore_wait(barrier, len(greet))

    def hop(src, slot, i, way, kind):
        at = pl.ds(*spans[i])
        dst = kvb.at[slot, kind, at]
        return remote(src.at[at], dst, kv_s.at[slot, i, kind], kv_r.at[slot, i, kind], ring[way])

    send_q = remote(q_ref, qin.at[1], q_s, q_r, z_mate)
    for i in (0, 1):
        for kind in (0, 1):
            for way in (0, 1):
                hop((k_ref, v_ref)[kind], 1 + way, i, way, kind).start()
        if i == 0:
            send_q.start()
    send_w = [
        remote(w_ref.at[:, wcols(b, 1 - co)], wbuf.at[b, co], w_s.at[b], w_r.at[b], core_mate)
        for b in range(nzh)
    ]
    for c in send_w:
        c.start()
    for c in local_w:
        c.start()
    send_r = remote(res_ref, resv, r_s, r_r, x_next)
    send_r.start()

    m_ref[...] = jnp.full(m_ref.shape, NEG, F32)
    l_ref[...] = jnp.zeros(l_ref.shape, F32)
    acc[...] = jnp.zeros(acc.shape, F32)
    lane_row = lax.broadcasted_iota(jnp.int32, (1, two), 1) % rows
    offset = off_ref[0]
    stat_row = lax.broadcasted_iota(jnp.int32, (16, two), 0)
    scale = HD ** (-0.5) * LOG2E

    def lay_queries(c):
        for g in (0, 1):
            for h in (0, 1):
                col = (2 * g + h) * HD
                qs[2 * c + g, h * rows : (h + 1) * rows, :] = qin[c, :, col : col + HD]

    def cross_hop(kind):
        at = pl.ds(*spans[1])
        return remote(
            kvb.at[ny - 2, kind, at], kvb.at[ny, kind, at], kv_s.at[ny, 1, kind], kv_r.at[ny, 1, kind], cross_to
        )

    def turn(slot, start, size):
        vt[slot, :, start : start + size] = kvb[slot, 1, start : start + size, :].T

    def attend(slot, block, start, size, first, last, side=0):
        key_pos = (block * 2 + zl + side * (1 - 2 * zl)) * klen + start + lax.broadcasted_iota(jnp.int32, (size, two), 0)

        def row_class(other, carry):
            row_pos = offset + (y * 2 + zl + other * (1 - 2 * zl)) * rows + lane_row
            visible = key_pos <= row_pos
            for g in (2 * other, 2 * other + 1):
                scores = lax.dot_general(
                    kvb[slot, 0, start : start + size, :], qs[g], (((1,), (1,)), ((), ())), preferred_element_type=F32
                )
                scores = jnp.where(visible, scores, NEG)
                top_old = m_ref[g]
                top = jnp.maximum(jnp.max(scores, axis=0, keepdims=True).astype(BF).astype(F32), top_old)
                weights = jnp.exp2((scores - top) * scale)
                fade = jnp.exp2((top_old - top) * scale)
                m_ref[g] = top
                l_ref[g] = l_ref[g] * fade + jnp.sum(weights, axis=0, keepdims=True)
                mixed = jnp.dot(
                    vt[slot, :, start : start + size], weights.astype(BF), preferred_element_type=F32
                )
                acc[g] = acc[g] * fade + mixed
            return carry

        lax.fori_loop(first, last, row_class, 0)

    def arrive(slot, i, way, kind):
        return hop(kvb.at[slot, kind], slot, i, way, kind)

    local_q.wait()
    lay_queries(0)
    local_k.wait()
    local_v.wait()
    turn(0, 0, klen)

    def forward(h, i, kind):
        for way in (0, 1):
            slot = 2 * h - 1 + way
            arrive(slot, i, way, kind).wait_recv()
            dest = 2 * h + 1 if way == 0 else jnp.minimum(2 * h + 2, ny - 1)
            onward = hop(kvb.at[slot, kind], dest, i, way, kind)
            if way == i:
                onward.start()
                if way == 1:

                    @pl.when(h == hops - 1)
                    def _():
                        cross_hop(kind).start()

            else:

                @pl.when(h < hops - 1)
                def _():
                    onward.start()

    def round_trip(h, carry):
        forward(h, 0, 0)

        @pl.when(h > 1)
        def _():
            attend(2 * h - 3, (y + ny + 1 - h) % ny, 0, klen, 1, 2)

        forward(h, 0, 1)

        @pl.when(h > 1)
        def _():
            turn(2 * h - 2, 0, klen)

        attend(2 * h - 2, (y + h - 1) % ny, 0, klen, 0, 1)
        forward(h, 1, 0)

        @pl.when(h == 1)
        def _():
            send_q.wait_recv()
            lay_queries(1)

        attend(2 * h - 2, (y + h - 1) % ny, 0, klen, 1, 2)
        forward(h, 1, 1)
        turn(2 * h - 1, 0, klen)
        attend(2 * h - 1, (y + ny - h) % ny, 0, klen, 0, 1)
        return carry

    lax.fori_loop(1, hops, round_trip, 0)

    last = ny - 1
    far_block = (y + hops) % ny
    attend(last - 2, (y + ny + 1 - hops) % ny, 0, klen, 1, 2)
    turn(last - 1, 0, klen)
    attend(last - 1, (y + hops - 1) % ny, 0, klen, 0, 2)
    for kind in (0, 1):
        arrive(last, 0, 0, kind).wait_recv()
    turn(last, 0, cut)
    attend(last, far_block, 0, cut, 1, 2)
    send_a = [remote(snd.at[g], rcv.at[g], a_s.at[g], a_r.at[g], z_mate) for g in (0, 1)]
    for g in (0, 1):
        snd[g, 0:HD, :] = acc[2 + g].astype(BF)
        total = l_ref[2 + g]
        high = total.astype(BF).astype(F32)
        packed = jnp.where(
            stat_row == 0,
            m_ref[2 + g],
            jnp.where(stat_row == 1, high, jnp.where(stat_row == 2, total - high, 0.0)),
        )
        snd[g, HD:, :] = packed.astype(BF)
        send_a[g].start()
    attend(last, far_block, 0, cut, 0, 1)
    for kind in (0, 1):
        arrive(last, 1, 1, kind).wait_recv()
    turn(last, cut, klen - cut)
    attend(last, far_block, cut, klen - cut, 0, 1)
    for kind in (0, 1):
        cross_hop(kind).wait_recv()
    turn(ny, cut, klen - cut)
    attend(ny, far_block, cut, klen - cut, 0, 1, 1)
    for g in (0, 1):
        send_a[g].wait_recv()
        stats = rcv[g, HD:, :].astype(F32)
        top_in = stats[0:1]
        sum_in = stats[1:2] + stats[2:3]
        top_new = jnp.maximum(top_in, m_ref[g])
        f_in = jnp.exp2((top_in - top_new) * scale)
        f_own = jnp.exp2((m_ref[g] - top_new) * scale)
        sum_new = sum_in * f_in + l_ref[g] * f_own
        head = (rcv[g, 0:HD, :].astype(F32) * f_in + acc[g] * f_own) / sum_new
        for h in (0, 1):
            col = (2 * g + h) * HD
            att[co, :, col : col + HD] = head[:, h * rows : (h + 1) * rows].T.astype(BF)

    send_t = remote(att.at[co], att.at[co], t_s, t_r, core_mate)
    send_t.start()
    for c in local_w:
        c.wait()
    for c in send_w:
        c.wait_recv()

    def share(core, away):
        return jnp.dot(att[core], wbuf[(zh + away) % nzh, core], preferred_element_type=F32)

    first_half = share(co, 2)
    send_t.wait_recv()

    def product(away):
        return share(0, away) + share(1, away)

    def span(i, j):
        return slice(i * half + j * part, i * half + (j + 1) * part)

    far_cp = [[remote(far_s.at[i, j], far_r.at[i, j], far_ss.at[i, j], far_rs.at[i, j], zring[i]) for j in range(PARTS)] for i in (0, 1)]
    near_cp = [[remote(near_s.at[i, j], near_r.at[i, j], near_ss.at[i, j], near_rs.at[i, j], landing[i]) for j in range(PARTS)] for i in (0, 1)]
    mix_cp = [[remote(mix_s.at[i, j], mix_r.at[i, j], mix_ss.at[i, j], mix_rs.at[i, j], landing[i]) for j in range(PARTS)] for i in (0, 1)]
    own_cp = [[remote(own_s.at[i, j], own_r.at[i, j], own_ss.at[i, j], own_rs.at[i, j], x_next) for j in range(PARTS)] for i in (0, 1)]
    out_cp = [[pltpu.make_async_copy(fin.at[span(i, j)], o_ref.at[span(i, j)], o_l.at[i, j]) for j in range(PARTS)] for i in (0, 1)]

    opposite = first_half + share(1 - co, 2)
    for j in range(PARTS):
        for i in (0, 1):
            far_s[i, j] = opposite[span(i, j)].astype(BF)
            far_cp[i][j].start()
    own = product(0)
    for j in range(PARTS):
        for i in (0, 1):
            own_s[i, j] = own[span(i, j)].astype(BF)
            own_cp[i][j].start()
    for i in (0, 1):
        out = product(1 if i == 0 else nzh - 1)
        keep[i] = out[i * half : (i + 1) * half]
        for j in range(PARTS):
            near_s[i, j] = out[span(1 - i, j)].astype(BF)
            near_cp[i][j].start()
    for j in range(PARTS):
        for i in (0, 1):
            far_cp[i][j].wait_recv()
            mix_s[i, j] = (keep[i, j * part : (j + 1) * part] + far_r[i, j].astype(F32)).astype(BF)
            mix_cp[i][j].start()
    send_r.wait_recv()
    for j in range(PARTS):
        for i in (0, 1):
            own_cp[i][j].wait_recv()
            near_cp[1 - i][j].wait_recv()
            mix_cp[i][j].wait_recv()
            summed = own_r[i, j].astype(F32) + near_r[1 - i, j].astype(F32) + mix_r[i, j].astype(F32)
            fin[span(i, j)] = (resv[span(i, j)].astype(F32) + summed).astype(BF)
            out_cp[i][j].start()

    send_q.wait_send()
    send_r.wait_send()
    for c in send_w:
        c.wait_send()
    send_t.wait_send()
    for c in send_a:
        c.wait_send()

    def drain(slot, carry):
        for i in (0, 1):
            for kind in (0, 1):
                arrive(slot, i, 0, kind).wait_send()
        return carry

    lax.fori_loop(1, ny, drain, 0)
    for kind in (0, 1):
        cross_hop(kind).wait_send()
    for i in (0, 1):
        for j in range(PARTS):
            far_cp[i][j].wait_send()
            own_cp[i][j].wait_send()
            near_cp[i][j].wait_send()
            mix_cp[i][j].wait_send()
            out_cp[i][j].wait()


def on_device(ny, nzh, nx, row_offsets, queries, cache_keys, cache_values, residual, out_weight):
    q, k, v, res, w = queries[0], cache_keys[0], cache_values[0], residual[0], out_weight[0]
    rows, klen, width = q.shape[0], k.shape[0], res.shape[1]
    half = rows // 2
    part = half // PARTS
    dma = pltpu.SemaphoreType.DMA
    piece = pltpu.VMEM((2, PARTS, part, width), BF)
    any_spec = pl.BlockSpec(memory_space=pl.ANY)
    out = pl.pallas_call(
        functools.partial(kernel, ny, nzh, nx),
        out_shape=jax.ShapeDtypeStruct(res.shape, BF),
        in_specs=[pl.BlockSpec(memory_space=pltpu.SMEM)] + [any_spec] * 5,
        out_specs=any_spec,
        scratch_shapes=[
            pltpu.VMEM((ny + 1, 2, klen, HD), BF),
            pltpu.VMEM((ny + 1, HD, klen), BF),
            pltpu.VMEM((2, rows, G * HD), BF),
            pltpu.VMEM((4, 2 * rows, HD), BF),
            pltpu.VMEM((4, 1, 2 * HD), F32),
            pltpu.VMEM((4, 1, 2 * HD), F32),
            pltpu.VMEM((4, HD, 2 * HD), F32),
            pltpu.VMEM((2, HD + 16, 2 * HD), BF),
            pltpu.VMEM((2, HD + 16, 2 * HD), BF),
            pltpu.VMEM((2, rows, G * HD), BF),
            pltpu.VMEM((nzh, 2, w.shape[0], width), BF),
            pltpu.VMEM((rows, width), BF),
            pltpu.VMEM((2, half, width), F32),
            piece, piece, piece, piece, piece, piece, piece, piece,
            pltpu.VMEM((rows, width), BF),
            dma((3,)), dma((ny + 1, 2, 2)), dma((ny + 1, 2, 2)),
            dma(()), dma(()), dma((2,)), dma((2,)),
            dma((nzh,)), dma((nzh,)), dma((nzh,)),
            dma(()), dma(()),
            dma((2, PARTS)), dma((2, PARTS)), dma((2, PARTS)), dma((2, PARTS)), dma((2, PARTS)), dma((2, PARTS)),
            dma((2, PARTS)), dma((2, PARTS)), dma(()), dma(()), dma((2, PARTS)),
        ],
        compiler_params=pltpu.CompilerParams(
            collective_id=0, has_side_effects=True, vmem_limit_bytes=64 * 1024 * 1024 - 70000
        ),
    )(row_offsets, q, k, v, res, w)
    return out[None]


def solution(mesh):
    placed = (
        P("section"),
        P("section", "ctx", "tp"),
        P("section", "ctx", "tp"),
        P("section", "ctx", "tp"),
        P("section", "ctx", "tp"),
        P("section", "tp", None),
    )
    ny, nzh, nx = mesh.shape["ctx"] // 2, mesh.shape["tp"] // 2, mesh.shape["section"]
    return jax.shard_map(
        functools.partial(on_device, ny, nzh, nx),
        mesh=mesh, in_specs=placed, out_specs=P("section", "ctx", "tp"), check_vma=False,
    )
```
